128 devices in a mesh: dp: 4 (over z), rows: 32 (over x, y, core).
Axes of the slice: x: 4, y: 4, z: 4, core: 2. Of those that a mesh axis runs over, the one named last changes fastest.
Arguments:
- owners: int32 [131072, 1], P(('dp', 'rows')), may hold values from 0 to 127; in each aligned block of 1024 rows (0 to 1023, 1024 to 2047, ...) at most 32 rows name the same one
- offsets: int32 [131072], P(('dp', 'rows')), may hold values from 0 to 8191
- gradients: bfloat16 [131072, 128], P(('dp', 'rows')), may hold values from -6 to 6
- embedding: float32 [1048576, 128], P(('dp', 'rows')), may hold values from -6 to 6
- adagrad_state: float32 [1048576], P(('dp', 'rows')), may hold values from 0.05 to 2
- next_owners: int32 [131072, 1], P(('dp', 'rows')), may hold values from 0 to 127; in each aligned block of 1024 rows (0 to 1023, 1024 to 2047, ...) at most 32 rows name the same one
- next_offsets: int32 [131072], P(('dp', 'rows')), may hold values from 0 to 8191
Outputs:
- new_embedding: float32 [1048576, 128], P(('dp', 'rows'))
- new_state: float32 [1048576], P(('dp', 'rows'))
- next_rows: bfloat16 [131072, 128], P(('dp', 'rows'))
The draws below stay inside these ranges and needn't reach their ends.
Inputs may be any that keep to these rules, and one draw needn't show every extreme that they name: `owners`: within the 1024 rows of one device, at most 32 rows name the same block. `next_owners`: within the 1024 rows of one device, at most 32 rows name the same block.
All inputs are finite; a program needn't handle non-finite values.
Results may differ from the reference program's by a relative error of at most 0.0013.
Values may be sent and summed in bfloat16 or wider, within the bound.
No kernel may reach another device: no remote copies, remote signals or barrier semaphores. Data moves between devices by JAX's collectives and lax.ppermute only.
A program may use at most 64 MiB of HBM per device.

```python
import math
import jax
import jax.numpy as jnp
import numpy as np
from jax import lax

W = 128
R_DEV = 8192
L_DEV = 1024
V = 1048576
LOOKUPS = 131072
CAP = 32
N_DP = 4
N_ROWS = 32


def plant(result, own_key, low, top_value):
    longest = result.shape.index(max(result.shape))
    spots = []
    for shift in (0, 1):
        where = [jax.random.randint(jax.random.fold_in(own_key, axis), (), 0, length) for axis, length in enumerate(result.shape)]
        where[longest] = (where[longest] + shift) % result.shape[longest]
        spots.append(tuple(where))
    return result.at[spots[0]].set(low).at[spots[1]].set(top_value)


def levels(own_key, extent, cuts, least, top_value):
    gain, own = 1.0, jax.random.fold_in(own_key, 6)
    for position, parts in cuts:
        steps = jnp.exp(jax.random.uniform(jax.random.fold_in(own, position), (parts,), jnp.float32, least / len(cuts), top_value / len(cuts)))
        gain = gain * jnp.repeat(steps, extent[position] // parts).reshape([-1 if axis == position else 1 for axis in range(len(extent))])
    return gain


def cumulative_ranks(count, lean):
    loads = [(1 << 20) // math.isqrt(rank ** lean) + 1 for rank in range(1, count + 1)]
    deviation = 1 + sum(loads) // (1 << 30)
    return np.cumsum(np.array([max(1, weight // deviation) for weight in loads]))


def ranked_ids(rng, dims, count, slope):
    listing = cumulative_ranks(count, slope)
    ticket = jax.random.randint(jax.random.fold_in(rng, 1), dims, 0, int(listing[count - 1]))
    rank = jnp.searchsorted(jnp.asarray(listing, jnp.int32), ticket, side="right")
    return jax.random.permutation(jax.random.fold_in(rng, 2), count)[rank].astype(jnp.int32)


def deal_out(stream_key, own, number, rows, count, top, bound, skew):
    sequence = jax.random.permutation(stream_key, count)
    packed, common = portions_of(count, rows * top, bound, skew, True), portions_of(count, rows * top, bound, skew, False)
    places = jnp.arange(count)

    def named(lengths, rotation):
        used = int((lengths > 0).sum())
        fixed = max(1, used // 4)
        shifted = fixed + (places - fixed + rotation * (used - fixed)) % max(1, count - fixed)
        return jnp.zeros((count,), jnp.int32).at[sequence[jnp.where(places < fixed, places, shifted)]].set(jnp.asarray(lengths, jnp.int32))

    lengths = jnp.where(number % 4 == 0, named(packed, number // 4), named(common, number - number // 4 - 1))
    mixed = jax.random.permutation(jax.random.fold_in(own, 3), count)
    giver, receiver = mixed[0:count // 2 * 2:2], mixed[1:count // 2 * 2:2]
    room = jnp.minimum(lengths[giver] - 1, bound - lengths[receiver]) // 2
    room = jnp.where((giver == sequence[0]) | (receiver == sequence[0]) | (lengths[receiver] == 0), 0, jnp.maximum(room, 0))
    shifted = jax.random.randint(jax.random.fold_in(own, 4), (count // 2,), 0, 1 << 20) % (room + 1)
    lengths = lengths.at[giver].add(-shifted).at[receiver].add(shifted)
    items = jnp.searchsorted(jnp.cumsum(lengths), jnp.arange(rows * top), side="right").astype(jnp.int32)
    grid = items.reshape(top, rows).T
    grid = grid[jax.random.permutation(jax.random.fold_in(own, 1), rows)]
    rotation = jax.random.randint(jax.random.fold_in(own, 2), (rows, 1), 0, top)
    return jnp.take_along_axis(grid, (jnp.arange(top)[None, :] + rotation) % top, axis=1)


def portions_of(count, total, bound, lean, full):
    portions = [(1 << 20) // math.isqrt(standing ** lean) + 1 for standing in range(1, count + 1)]
    largest = bound if full else min(bound, max(-(-total // count), total * portions[0] // sum(portions)))
    least = 1 if total - largest >= count - 1 else 0
    counts, spare = [largest] + [least] * (count - 1), total - largest - least * (count - 1)
    while spare > 0:
        movable = [i for i in range(1, count) if counts[i] < largest] or [i for i in range(1, count) if counts[i] < bound]
        pool, budget = sum([portions[i] for i in movable]), spare
        for i in movable:
            extra = min(bound - counts[i], max(1, budget * portions[i] // pool), spare)
            counts[i] = counts[i] + extra
            spare = spare - extra
    return np.array(counts)


def centred(rng, dims, spread, most, cuts=(), dtype=jnp.bfloat16):
    values = jax.random.normal(rng, dims, jnp.float32) * spread
    if len(cuts) > 0:
        values = levels(rng, dims, cuts, -0.22, 0.18) * values
    return jnp.clip(values, min=-most, max=most).astype(dtype)


def setup_inputs(seed: int = 0) -> dict:
    key_list = jax.random.split(jax.random.key(seed), 8)
    owners_keys = jax.random.split(jax.random.fold_in(key_list[0], 1), LOOKUPS // L_DEV)
    owners_turns = jax.random.permutation(jax.random.fold_in(key_list[0], 3), LOOKUPS // L_DEV)
    owners = jax.vmap(lambda own, number: deal_out(jax.random.fold_in(key_list[0], 2), own, number, L_DEV, N_DP * N_ROWS, 1, CAP, 2))(owners_keys, owners_turns).reshape((LOOKUPS, 1))
    offsets = plant(ranked_ids(key_list[1], (LOOKUPS,), R_DEV, 2), jax.random.fold_in(key_list[1], 3), 0, R_DEV - 1).astype(jnp.int32)
    gradients = centred(key_list[2], (LOOKUPS, W), 1.0, 6.0, ((0, 128),))
    embedding = centred(key_list[3], (V, W), 1.0, 6.0, ((0, 128),), jnp.float32)
    adagrad_state = jnp.clip(jnp.exp(math.log(2.0) - 3.6888794 * jax.random.uniform(key_list[4], (V,), jnp.float32) ** levels(key_list[4], (V,), ((0, 128),), -0.2, 0.2)), 0.05, 2.0)
    next_owners_keys = jax.random.split(jax.random.fold_in(key_list[5], 1), LOOKUPS // L_DEV)
    next_owners_turns = jax.random.permutation(jax.random.fold_in(key_list[5], 3), LOOKUPS // L_DEV)
    next_owners = jax.vmap(lambda own, number: deal_out(jax.random.fold_in(key_list[5], 2), own, number, L_DEV, N_DP * N_ROWS, 1, CAP, 2))(next_owners_keys, next_owners_turns).reshape((LOOKUPS, 1))
    next_offsets = plant(ranked_ids(key_list[6], (LOOKUPS,), R_DEV, 2), jax.random.fold_in(key_list[6], 3), 0, R_DEV - 1).astype(jnp.int32)
    return {"owners": owners, "offsets": offsets, "gradients": gradients, "embedding": embedding, "adagrad_state": adagrad_state, "next_owners": next_owners, "next_offsets": next_offsets}


def reference(owners, offsets, gradients, embedding, adagrad_state, next_owners, next_offsets):
    row_ids = (owners[:, 0] * R_DEV + offsets).astype(jnp.int32)
    grad_sum = jnp.zeros((V, W), jnp.float32).at[row_ids].add(gradients.astype(jnp.float32))
    new_state = adagrad_state + lax.optimization_barrier(jnp.mean(grad_sum * grad_sum, axis=1))
    new_embedding = embedding - 0.5 * grad_sum / jnp.sqrt(new_state)[:, None]
    next_ids = (next_owners[:, 0] * R_DEV + next_offsets).astype(jnp.int32)
    next_rows = new_embedding[next_ids].astype(jnp.bfloat16)
    return (new_embedding, new_state, next_rows)
```

```python
import functools

import jax
import jax.numpy as jnp
from jax import lax
from jax.experimental import pallas as pl
from jax.experimental.pallas import tpu as pltpu
from jax.sharding import PartitionSpec as P

AXES = ("dp", "rows")
F32, BF16, I32 = jnp.float32, jnp.bfloat16, jnp.int32
LANES = 128
TABLES = 4


def iota(shape, dim):
    return lax.broadcasted_iota(I32, shape, dim)


def pack_kernel(cap, rows_out, own_ref, off_ref, nown_ref, noff_ref, g_ref, out_ref, q_ref,
                gf, outf, pos_v, pos_s, sem):
    blocks = own_ref.shape[0]
    devices = out_ref.shape[0]
    before = (iota((LANES, LANES), 0) < iota((LANES, LANES), 1)).astype(BF16)
    ones = jnp.ones((LANES, LANES), BF16)
    row = iota((LANES, LANES), 0)
    meta = jnp.zeros((devices, LANES), F32)

    def slots(o_ref, f_ref, first, meta):
        base = jnp.zeros((devices, LANES), F32)
        out = []
        for b in range(blocks):
            own = o_ref[b:b + 1, :]
            hit = iota((devices, LANES), 0) == own
            hot = hit.astype(BF16)
            ahead = jnp.dot(hot, before, preferred_element_type=F32) + base
            slot = jnp.sum(jnp.where(hit, ahead, 0.0), axis=0, keepdims=True).astype(I32)
            base = base + jnp.dot(hot, ones, preferred_element_type=F32)
            off = f_ref[b:b + 1, :]
            value = jnp.where(row < first + cap, off // LANES, off % LANES)
            here = (row >= first) & (row < first + 2 * cap) & (row % cap == slot)
            sel = jnp.where(here, value, 0).astype(F32).astype(BF16)
            meta = meta + lax.dot_general(hot, sel, (((1,), (1,)), ((), ())), preferred_element_type=F32)
            out.append((own, slot))
        return out, meta

    got, meta = slots(own_ref, off_ref, 0, meta)
    for b, (own, slot) in enumerate(got):
        pos_v[b:b + 1, :] = own * rows_out + slot
    copy = pltpu.make_async_copy(pos_v, pos_s, sem)
    copy.start()
    gf[...] = g_ref[...].astype(F32)
    outf[...] = jnp.zeros_like(outf)
    got, meta = slots(nown_ref, noff_ref, 2 * cap, meta)
    for b, (own, slot) in enumerate(got):
        q_ref[b:b + 1, :] = own * cap + slot
    outf[pl.ds(cap, devices, stride=rows_out), :] = meta
    copy.wait()

    for b in range(blocks):
        def step(i, carry, b=b):
            for k in range(16):
                j = i * 16 + k
                outf[pl.ds(pos_s[b, j], 1), :] = gf[pl.ds(b * LANES + j, 1), :]
            return carry
        lax.fori_loop(0, LANES // 16, step, 0)

    def narrow(d, carry):
        out_ref[d] = outf[pl.ds(pl.multiple_of(d * rows_out, 8), rows_out), :].astype(BF16)
        return carry
    lax.fori_loop(0, devices, narrow, 0, unroll=4)


def owner_kernel(cap, inc_ref, state_ref, emb_hbm, nemb_hbm, nstate_ref, ret_ref,
                 t0, t1, t2, t3, gf, metaf, idx_v, idx_s, emb, sems):
    devices, rows_in, columns = inc_ref.shape
    owned = emb.shape[0]
    tabs = (t0, t1, t2, t3)
    load = pltpu.make_async_copy(emb_hbm, emb, sems.at[0])
    load.start()

    def spread(d, carry):
        metaf[pl.ds(pl.multiple_of(d * 8, 8), 8), :] = inc_ref[d, cap:cap + 8, :].astype(F32)
        return carry
    lax.fori_loop(0, devices, spread, 0, unroll=8)
    m = metaf[pl.ds(0, devices, stride=8), :]
    idx_v[...] = (m * LANES + pltpu.roll(m, LANES - cap, 1)).astype(I32)
    copy = pltpu.make_async_copy(idx_v, idx_s, sems.at[1])
    copy.start()

    def widen(d, carry):
        gf[pl.ds(pl.multiple_of(d * cap, 8), cap), :] = inc_ref[d, 0:cap, :].astype(F32)
        return carry
    lax.fori_loop(0, devices, widen, 0, unroll=4)

    def clear(c, carry):
        for t in tabs:
            t[pl.ds(pl.multiple_of(c * 64, 64), 64), :] = jnp.zeros((64, columns), F32)
        return carry
    lax.fori_loop(0, owned // 64, clear, 0)
    copy.wait()

    def add(d, carry):
        for i in range(0, cap, TABLES):
            at = [pl.ds(idx_s[d, i + k], 1) for k in range(TABLES)]
            new = [tabs[k][at[k], :] + gf[pl.ds(d * cap + i + k, 1), :] for k in range(TABLES)]
            for k in range(TABLES):
                tabs[k][at[k], :] = new[k]
        return carry
    lax.fori_loop(0, devices, add, 0)
    load.wait()

    ones = jnp.ones((8, columns), BF16)
    per = 4
    nt = (((1,), (1,)), ((), ()))

    def update(c, carry):
        rows = pl.ds(pl.multiple_of(c * per * LANES, per * LANES), per * LANES)
        total = (t0[rows, :] + t1[rows, :]) + (t2[rows, :] + t3[rows, :])
        square = total * total
        high = square.astype(BF16)
        low = (square - high.astype(F32)).astype(BF16)
        mean = (lax.dot_general(ones, high, nt, preferred_element_type=F32)
                + lax.dot_general(ones, low, nt, preferred_element_type=F32)) * (1.0 / columns)
        for k in range(per):
            state = state_ref[pl.ds(c * per + k, 1), :] + mean[0:1, k * LANES:(k + 1) * LANES]
            nstate_ref[pl.ds(c * per + k, 1), :] = state
            scale = jnp.transpose(jnp.broadcast_to(0.5 / jnp.sqrt(state), (LANES, LANES)))
            here = pl.ds(pl.multiple_of((c * per + k) * LANES, LANES), LANES)
            emb[here, :] = emb[here, :] - total[k * LANES:(k + 1) * LANES, :] * scale
        pltpu.make_async_copy(emb.at[rows, :], nemb_hbm.at[rows, :], sems.at[2]).start()
        return carry
    lax.fori_loop(0, owned // (per * LANES), update, 0)

    def fetch(d, carry):
        for i in range(cap):
            gf[pl.ds(d * cap + i, 1), :] = emb[pl.ds(idx_s[d, 2 * cap + i], 1), :]
        return carry
    lax.fori_loop(0, devices, fetch, 0)

    def narrow(d, carry):
        ret_ref[d] = gf[pl.ds(pl.multiple_of(d * cap, 8), cap), :].astype(BF16)
        return carry
    lax.fori_loop(0, devices, narrow, 0, unroll=4)
    pltpu.make_async_copy(emb, nemb_hbm, sems.at[2]).wait()


def unpack_kernel(cap, q_ref, ret_ref, out_ref, wide, rows):
    devices = ret_ref.shape[0]

    def widen(d, carry):
        wide[pl.ds(pl.multiple_of(d * cap, 8), cap), :] = ret_ref[d].astype(F32)
        return carry
    lax.fori_loop(0, devices, widen, 0, unroll=4)
    for b in range(q_ref.shape[0]):
        def step(i, carry, b=b):
            for k in range(16):
                j = i * 16 + k
                rows[pl.ds(b * LANES + j, 1), :] = wide[pl.ds(q_ref[b, j], 1), :]
            return carry
        lax.fori_loop(0, LANES // 16, step, 0)
    out_ref[...] = rows[...].astype(BF16)


VM = pl.BlockSpec(memory_space=pltpu.VMEM)
SM = pl.BlockSpec(memory_space=pltpu.SMEM)
ANY = pl.BlockSpec(memory_space=pl.ANY)


def on_device(owners, offsets, gradients, embedding, adagrad_state, next_owners, next_offsets):
    devices = lax.axis_size(AXES)
    lookups, columns = gradients.shape
    owned = embedding.shape[0]
    cap = max(2, 4 * lookups // devices)
    rows_out = cap + 8
    blocks = lookups // LANES
    shape = jax.ShapeDtypeStruct
    view = lambda x: x.reshape(blocks, LANES)

    outgoing, q = pl.pallas_call(
        functools.partial(pack_kernel, cap, rows_out),
        out_shape=(shape((devices, rows_out, columns), BF16), shape((blocks, LANES), I32)),
        in_specs=[VM] * 5,
        out_specs=(VM, VM),
        scratch_shapes=[
            pltpu.VMEM((lookups, columns), F32),
            pltpu.VMEM((devices * rows_out, columns), F32),
            pltpu.VMEM((blocks, LANES), I32),
            pltpu.SMEM((blocks, LANES), I32),
            pltpu.SemaphoreType.DMA,
        ],
        name="pack",
    )(view(owners), view(offsets), view(next_owners), view(next_offsets), gradients)

    incoming = lax.all_to_all(outgoing, AXES, split_axis=0, concat_axis=0, tiled=True)

    new_embedding, new_state, fetched = pl.pallas_call(
        functools.partial(owner_kernel, cap),
        out_shape=(
            shape(embedding.shape, F32),
            shape((owned // LANES, LANES), F32),
            shape((devices, cap, columns), BF16),
        ),
        in_specs=[VM, VM, ANY],
        out_specs=(ANY, VM, VM),
        scratch_shapes=[pltpu.VMEM((owned, columns), F32)] * TABLES
        + [
            pltpu.VMEM((devices * cap, columns), F32),
            pltpu.VMEM((devices * 8, columns), F32),
            pltpu.VMEM((devices, LANES), I32),
            pltpu.SMEM((devices, LANES), I32),
            pltpu.VMEM((owned, columns), F32),
            pltpu.SemaphoreType.DMA((3,)),
        ],
        name="owner",
    )(incoming, adagrad_state.reshape(owned // LANES, LANES), embedding)

    returned = lax.all_to_all(fetched, AXES, split_axis=0, concat_axis=0, tiled=True)

    next_rows = pl.pallas_call(
        functools.partial(unpack_kernel, cap),
        out_shape=shape((lookups, columns), BF16),
        in_specs=[SM, VM],
        out_specs=VM,
        scratch_shapes=[
            pltpu.VMEM((devices * cap, columns), F32),
            pltpu.VMEM((lookups, columns), F32),
        ],
        name="unpack",
    )(q, returned)
    return (new_embedding, new_state.reshape(owned), next_rows)


def solution(mesh):
    line, block = P(AXES), P(AXES, None)
    return jax.shard_map(
        on_device,
        mesh=mesh,
        in_specs=(block, line, block, block, line, block, line),
        out_specs=(block, line, block),
        check_vma=False,
    )
```

```python
import functools

import jax
import jax.numpy as jnp
from jax import lax
from jax.experimental import pallas as pl
from jax.experimental.pallas import tpu as pltpu
from jax.sharding import PartitionSpec as P

AXES = ("dp", "rows")
F32, BF16, I32 = jnp.float32, jnp.bfloat16, jnp.int32
LANES = 128
TABLES = 4


def iota(shape, dim):
    return lax.broadcasted_iota(I32, shape, dim)


def pack_kernel(cap, rows_out, own_hbm, off_hbm, nown_hbm, noff_hbm, g_hbm, out_ref, q_ref,
                own_ref, off_ref, nown_ref, noff_ref, g_ref, gf, outf, pos_v, pos_s, sems):
    loads = [
        pltpu.make_async_copy(src, dst, sems.at[k])
        for k, (src, dst) in enumerate((
            (own_hbm, own_ref), (off_hbm, off_ref), (nown_hbm, nown_ref), (noff_hbm, noff_ref), (g_hbm, g_ref)
        ))
    ]
    for load in loads:
        load.start()
    outf[...] = jnp.zeros_like(outf)
    blocks = own_ref.shape[0]
    devices = out_ref.shape[0] // rows_out
    before = (iota((LANES, LANES), 0) < iota((LANES, LANES), 1)).astype(BF16)
    ones = jnp.ones((LANES, LANES), BF16)
    row = iota((LANES, LANES), 0)
    meta = jnp.zeros((devices, LANES), F32)

    def slots(o_ref, f_ref, first, meta):
        base = jnp.zeros((devices, LANES), F32)
        out = []
        for b in range(blocks):
            own = o_ref[b:b + 1, :]
            hit = iota((devices, LANES), 0) == own
            hot = hit.astype(BF16)
            ahead = jnp.dot(hot, before, preferred_element_type=F32) + base
            slot = jnp.sum(jnp.where(hit, ahead, 0.0), axis=0, keepdims=True).astype(I32)
            base = base + jnp.dot(hot, ones, preferred_element_type=F32)
            off = f_ref[b:b + 1, :]
            value = jnp.where(row < first + cap, off // LANES, off % LANES)
            here = (row >= first) & (row < first + 2 * cap) & (row % cap == slot)
            sel = jnp.where(here, value, 0).astype(F32).astype(BF16)
            meta = meta + lax.dot_general(hot, sel, (((1,), (1,)), ((), ())), preferred_element_type=F32)
            out.append((own, slot))
        return out, meta

    loads[0].wait()
    loads[1].wait()
    got, meta = slots(own_ref, off_ref, 0, meta)
    for b, (own, slot) in enumerate(got):
        pos_v[b:b + 1, :] = own * rows_out + slot
    copy = pltpu.make_async_copy(pos_v, pos_s, sems.at[5])
    copy.start()
    for load in loads[2:]:
        load.wait()
    gf[...] = g_ref[...].astype(F32)
    got, meta = slots(nown_ref, noff_ref, 2 * cap, meta)
    for b, (own, slot) in enumerate(got):
        q_ref[b:b + 1, :] = own * cap + slot
    outf[pl.ds(cap, devices, stride=rows_out), :] = meta
    copy.wait()

    def place(b, carry):
        for j in range(LANES):
            outf[pl.ds(pos_s[b, j], 1), :] = gf[pl.ds(b * LANES + j, 1), :]
        return carry
    lax.fori_loop(0, blocks, place, 0)
    out_ref[...] = outf[...].astype(BF16)


def owner_kernel(cap, rows_in, inc_ref, state_hbm, emb_hbm, nemb_hbm, nstate_ref, ret_ref,
                 t0, t1, t2, t3, gf, idx_v, idx_s, emb, state_ref, sems):
    devices = idx_v.shape[0]
    owned, columns = emb.shape
    tabs = (t0, t1, t2, t3)
    gf[...] = inc_ref[...].astype(F32)
    m = gf[pl.ds(cap, devices, stride=rows_in), :]
    idx_v[...] = (m * LANES + pltpu.roll(m, LANES - cap, 1)).astype(I32)
    copy = pltpu.make_async_copy(idx_v, idx_s, sems.at[1])
    copy.start()

    def clear(c, carry):
        for t in tabs:
            t[pl.ds(pl.multiple_of(c * 64, 64), 64), :] = jnp.zeros((64, columns), F32)
        return carry
    lax.fori_loop(0, owned // 64, clear, 0)
    copy.wait()
    load = pltpu.make_async_copy(emb_hbm, emb, sems.at[0])
    load.start()
    load_state = pltpu.make_async_copy(state_hbm, state_ref, sems.at[3])
    load_state.start()

    def add(d, carry):
        for i in range(0, cap, TABLES):
            at = [pl.ds(idx_s[d, i + k], 1) for k in range(TABLES)]
            new = [tabs[k][at[k], :] + gf[pl.ds(d * rows_in + i + k, 1), :] for k in range(TABLES)]
            for k in range(TABLES):
                tabs[k][at[k], :] = new[k]
        return carry
    lax.fori_loop(0, devices, add, 0)
    load.wait()
    load_state.wait()

    ones = jnp.ones((8, columns), BF16)
    per = 4
    nt = (((1,), (1,)), ((), ()))

    def update(c, carry):
        rows = pl.ds(pl.multiple_of(c * per * LANES, per * LANES), per * LANES)
        total = (t0[rows, :] + t1[rows, :]) + (t2[rows, :] + t3[rows, :])
        square = total * total
        high = square.astype(BF16)
        low = (square - high.astype(F32)).astype(BF16)
        mean = (lax.dot_general(ones, high, nt, preferred_element_type=F32)
                + lax.dot_general(ones, low, nt, preferred_element_type=F32)) * (1.0 / columns)
        for k in range(per):
            state = state_ref[pl.ds(c * per + k, 1), :] + mean[0:1, k * LANES:(k + 1) * LANES]
            nstate_ref[pl.ds(c * per + k, 1), :] = state
            scale = jnp.transpose(jnp.broadcast_to(0.5 / jnp.sqrt(state), (LANES, LANES)))
            here = pl.ds(pl.multiple_of((c * per + k) * LANES, LANES), LANES)
            emb[here, :] = emb[here, :] - total[k * LANES:(k + 1) * LANES, :] * scale
        pltpu.make_async_copy(emb.at[rows, :], nemb_hbm.at[rows, :], sems.at[2]).start()
        return carry
    lax.fori_loop(0, owned // (per * LANES), update, 0)

    def fetch(d, carry):
        for i in range(cap):
            gf[pl.ds(d * cap + i, 1), :] = emb[pl.ds(idx_s[d, 2 * cap + i], 1), :]
        return carry
    lax.fori_loop(0, devices, fetch, 0)

    ret_ref[...] = gf[0:devices * cap, :].astype(BF16)
    pltpu.make_async_copy(emb, nemb_hbm, sems.at[2]).wait()


def unpack_kernel(q_any, ret_ref, out_ref, wide, rows, q_ref, sem):
    copy = pltpu.make_async_copy(q_any, q_ref, sem)
    copy.start()
    wide[...] = ret_ref[...].astype(F32)
    copy.wait()

    def take(b, carry):
        for j in range(LANES):
            rows[pl.ds(b * LANES + j, 1), :] = wide[pl.ds(q_ref[b, j], 1), :]
        return carry
    lax.fori_loop(0, q_ref.shape[0], take, 0)
    out_ref[...] = rows[...].astype(BF16)


VM = pl.BlockSpec(memory_space=pltpu.VMEM)
ANY = pl.BlockSpec(memory_space=pl.ANY)


def on_device(owners, offsets, gradients, embedding, adagrad_state, next_owners, next_offsets):
    devices = lax.axis_size(AXES)
    lookups, columns = gradients.shape
    owned = embedding.shape[0]
    cap = max(2, 4 * lookups // devices)
    rows_out = cap + 2
    blocks = lookups // LANES
    shape = jax.ShapeDtypeStruct
    view = lambda x: x.reshape(blocks, LANES)
    in_hbm = lambda x: pltpu.with_memory_space_constraint(x, pltpu.HBM)

    outgoing, q = pl.pallas_call(
        functools.partial(pack_kernel, cap, rows_out),
        out_shape=(shape((devices * rows_out, columns), BF16), shape((blocks, LANES), I32)),
        in_specs=[ANY] * 5,
        out_specs=(VM, VM),
        scratch_shapes=[pltpu.VMEM((blocks, LANES), I32)] * 4
        + [
            pltpu.VMEM((lookups, columns), BF16),
            pltpu.VMEM((lookups, columns), F32),
            pltpu.VMEM((devices * rows_out, columns), F32),
            pltpu.VMEM((blocks, LANES), I32),
            pltpu.SMEM((blocks, LANES), I32),
            pltpu.SemaphoreType.DMA((6,)),
        ],
        compiler_params=pltpu.CompilerParams(vmem_limit_bytes=12 << 20),
        name="pack",
    )(*map(in_hbm, (view(owners), view(offsets), view(next_owners), view(next_offsets), gradients)))

    def exchange(x, pairs):
        x = x.reshape(devices, pairs, 2, columns)
        x = lax.all_to_all(x, AXES, split_axis=0, concat_axis=0, tiled=True)
        return x.reshape(devices * pairs * 2, columns)

    incoming = exchange(outgoing, rows_out // 2)

    new_embedding, new_state, fetched = pl.pallas_call(
        functools.partial(owner_kernel, cap, rows_out),
        out_shape=(
            shape(embedding.shape, F32),
            shape((owned // LANES, LANES), F32),
            shape((devices * cap, columns), BF16),
        ),
        in_specs=[VM, ANY, ANY],
        out_specs=(ANY, VM, VM),
        scratch_shapes=[pltpu.VMEM((owned, columns), F32)] * TABLES
        + [
            pltpu.VMEM((devices * rows_out, columns), F32),
            pltpu.VMEM((devices, LANES), I32),
            pltpu.SMEM((devices, LANES), I32),
            pltpu.VMEM((owned, columns), F32),
            pltpu.VMEM((owned // LANES, LANES), F32),
            pltpu.SemaphoreType.DMA((4,)),
        ],
        compiler_params=pltpu.CompilerParams(vmem_limit_bytes=36 << 20),
        name="owner",
    )(incoming, in_hbm(adagrad_state.reshape(owned // LANES, LANES)), in_hbm(embedding))

    returned = lax.all_to_all(
        fetched.reshape(devices, cap, columns), AXES, split_axis=0, concat_axis=0, tiled=True
    ).reshape(devices * cap, columns)

    next_rows = pl.pallas_call(
        unpack_kernel,
        out_shape=shape((lookups, columns), BF16),
        in_specs=[ANY, VM],
        out_specs=VM,
        scratch_shapes=[
            pltpu.VMEM((devices * cap, columns), F32),
            pltpu.VMEM((lookups, columns), F32),
            pltpu.SMEM((blocks, LANES), I32),
            pltpu.SemaphoreType.DMA,
        ],
        compiler_params=pltpu.CompilerParams(vmem_limit_bytes=12 << 20),
        name="unpack",
    )(q, returned)
    return (new_embedding, new_state.reshape(owned), next_rows)


def solution(mesh):
    line, block = P(AXES), P(AXES, None)
    return jax.shard_map(
        on_device,
        mesh=mesh,
        in_specs=(block, line, block, block, line, block, line),
        out_specs=(block, line, block),
        check_vma=False,
    )
```

```python
import functools

import jax
import jax.numpy as jnp
from jax import lax
from jax.experimental import pallas as pl
from jax.experimental.pallas import tpu as pltpu
from jax.sharding import PartitionSpec as P

AXES = ("dp", "rows")
F32, BF16, I32 = jnp.float32, jnp.bfloat16, jnp.int32
LANES = 128
TABLES = 4


def iota(shape, dim):
    return lax.broadcasted_iota(I32, shape, dim)


def pack_kernel(cap, rows_out, own_hbm, off_hbm, nown_hbm, noff_hbm, g_hbm, out_ref, q_ref,
                own_ref, off_ref, nown_ref, noff_ref, g_ref, gf, outf, pos_v, pos_s, sems):
    loads = [
        pltpu.make_async_copy(src, dst, sems.at[k])
        for k, (src, dst) in enumerate((
            (own_hbm, own_ref), (off_hbm, off_ref), (nown_hbm, nown_ref), (noff_hbm, noff_ref), (g_hbm, g_ref)
        ))
    ]
    for load in loads:
        load.start()
    outf[...] = jnp.zeros_like(outf)
    blocks = own_ref.shape[0]
    devices = out_ref.shape[0] // rows_out
    before = (iota((LANES, LANES), 0) < iota((LANES, LANES), 1)).astype(BF16)
    ones = jnp.ones((LANES, LANES), BF16)
    row = iota((LANES, LANES), 0)
    meta = jnp.zeros((devices, LANES), F32)

    def slots(o_ref, f_ref, first, meta):
        base = jnp.zeros((devices, LANES), F32)
        out = []
        for b in range(blocks):
            own = o_ref[b:b + 1, :]
            hit = iota((devices, LANES), 0) == own
            hot = hit.astype(BF16)
            ahead = jnp.dot(hot, before, preferred_element_type=F32) + base
            slot = jnp.sum(jnp.where(hit, ahead, 0.0), axis=0, keepdims=True).astype(I32)
            base = base + jnp.dot(hot, ones, preferred_element_type=F32)
            off = f_ref[b:b + 1, :]
            value = jnp.where(row < first + cap, off // LANES + 1, off % LANES)
            here = (row >= first) & (row < first + 2 * cap) & (row % cap == slot)
            sel = jnp.where(here, value, 0).astype(F32).astype(BF16)
            meta = meta + lax.dot_general(hot, sel, (((1,), (1,)), ((), ())), preferred_element_type=F32)
            out.append((own, slot))
        return out, meta

    loads[0].wait()
    loads[1].wait()
    got, meta = slots(own_ref, off_ref, 0, meta)
    pos_v[:, 0:blocks] = jnp.transpose(jnp.concatenate([own * rows_out + slot for own, slot in got], axis=0))
    copy = pltpu.make_async_copy(pos_v, pos_s, sems.at[5])
    copy.start()
    for load in loads[2:]:
        load.wait()
    gf[...] = g_ref[...].astype(F32)
    got, meta = slots(nown_ref, noff_ref, 2 * cap, meta)
    q_ref[:, 0:blocks] = jnp.transpose(jnp.concatenate([own * cap + slot for own, slot in got], axis=0))
    outf[pl.ds(cap, devices, stride=rows_out), :] = meta
    copy.wait()

    def place(b, carry):
        rows = gf.at[pl.ds(pl.multiple_of(b * LANES, LANES), LANES), :]
        for j in range(LANES):
            outf[pl.ds(pos_s.at[j][b], 1), :] = rows[j:j + 1, :]
        return carry
    lax.fori_loop(0, blocks, place, 0)
    out_ref[...] = outf[...].astype(BF16)


def pick(x, lane):
    return jnp.take_along_axis(x, jnp.full(x.shape, lane, I32), axis=1)


def owner_kernel(cap, rows_in, inc_ref, state_hbm, emb_hbm, nemb_hbm, nstate_hbm, ret_ref,
                 t0, t1, t2, t3, gf, idx_v, cols_v, emb, state_ref, nstate, scales, sems, idx_all):
    devices = idx_v.shape[1]
    owned, columns = emb.shape
    tabs = (t0, t1, t2, t3)
    gf[...] = inc_ref[...].astype(F32)
    m = gf[pl.ds(cap, devices, stride=rows_in), :]
    index = ((m - 1.0) * LANES + pltpu.roll(m, LANES - cap, 1)).astype(I32)
    apart = iota((devices, LANES), 0) * cap + iota((devices, LANES), 1) % cap
    idx_v[...] = jnp.transpose(jnp.where(index < 0, apart % owned, index))
    slots = list(range(cap)) + list(range(2 * cap, 3 * cap))
    copy = pltpu.make_async_copy(idx_v, idx_all, sems.at[1])
    copy.start()
    idx_s = [idx_all.at[i] for i in slots]
    load = pltpu.make_async_copy(emb_hbm, emb, sems.at[0])
    load.start()
    load_state = pltpu.make_async_copy(state_hbm, state_ref, sems.at[3])
    load_state.start()

    def clear(c, carry):
        for t in tabs:
            t[pl.ds(pl.multiple_of(c * 64, 64), 64), :] = jnp.zeros((64, columns), F32)
        return carry
    lax.fori_loop(0, owned // 64, clear, 0)
    copy.wait()

    def add(d, carry):
        rows = gf.at[pl.ds(d * rows_in, rows_in), :]
        for i in range(0, cap, TABLES):
            at = [pl.ds(idx_s[i + k][d], 1) for k in range(TABLES)]
            new = [tabs[k][at[k], :] + rows[i + k:i + k + 1, :] for k in range(TABLES)]
            for k in range(TABLES):
                tabs[k][at[k], :] = new[k]
        return carry
    lax.fori_loop(0, devices, add, 0)
    load_state.wait()

    eye = iota((LANES, LANES), 0) == iota((LANES, LANES), 1)
    per = 8

    def measure(c, carry):
        means = []
        for k in range(per):
            rows = pl.ds(pl.multiple_of((c * per + k) * LANES, LANES), LANES)
            total = (t0[rows, :] + t1[rows, :]) + (t2[rows, :] + t3[rows, :])
            t0[rows, :] = total
            square = total * total
            if k % 2:
                mean = jnp.sum(square, axis=1, keepdims=True)
                means.append(jnp.sum(jnp.where(eye, mean, 0.0), axis=0, keepdims=True))
            else:
                high = square.astype(BF16)
                low = (square - high.astype(F32)).astype(BF16)
                both = lax.dot_general(
                    jnp.ones((8, 2 * columns), BF16), jnp.concatenate([high, low], axis=1),
                    (((1,), (1,)), ((), ())), preferred_element_type=F32,
                )
                means.append(both[0:1, :])
        here = pl.ds(pl.multiple_of(c * per, per), per)
        state = state_ref[here, :] + jnp.concatenate(means, axis=0) * (1.0 / columns)
        nstate[here, :] = state
        scales[here, :] = 0.5 / jnp.sqrt(state)
        return carry
    lax.fori_loop(0, owned // (per * LANES), measure, 0)
    out_state = pltpu.make_async_copy(nstate, nstate_hbm, sems.at[3])
    out_state.start()
    load.wait()

    cols_v[:, 0:owned // LANES] = jnp.transpose(scales[...])
    def update(c, carry):
        for k in range(8):
            rows = pl.ds(pl.multiple_of((c * 8 + k) * LANES, LANES), LANES)
            emb[rows, :] = emb[rows, :] - t0[rows, :] * pick(cols_v[...], c * 8 + k)
        rows = pl.ds(pl.multiple_of(c * 8 * LANES, 8 * LANES), 8 * LANES)
        pltpu.make_async_copy(emb.at[rows, :], nemb_hbm.at[rows, :], sems.at[2]).start()
        return carry
    lax.fori_loop(0, owned // (8 * LANES), update, 0)

    def fetch(d, carry):
        rows = gf.at[pl.ds(pl.multiple_of(d * cap, cap), cap), :]
        for i in range(cap):
            rows[i:i + 1, :] = emb[pl.ds(idx_s[cap + i][d], 1), :]
        return carry
    lax.fori_loop(0, devices, fetch, 0)
    ret_ref[...] = gf[0:devices * cap, :].astype(BF16)
    out_state.wait()
    pltpu.make_async_copy(emb, nemb_hbm, sems.at[2]).wait()


def unpack_kernel(q_any, ret_ref, out_ref, wide, rows, q_ref, sem):
    copy = pltpu.make_async_copy(q_any, q_ref, sem)
    copy.start()
    wide[...] = ret_ref[...].astype(F32)
    copy.wait()

    def take(b, carry):
        here = rows.at[pl.ds(pl.multiple_of(b * LANES, LANES), LANES), :]
        for j in range(LANES):
            here[j:j + 1, :] = wide[pl.ds(q_ref.at[j][b], 1), :]
        return carry
    lax.fori_loop(0, out_ref.shape[0] // LANES, take, 0)
    out_ref[...] = rows[...].astype(BF16)


VM = pl.BlockSpec(memory_space=pltpu.VMEM)
ANY = pl.BlockSpec(memory_space=pl.ANY)


def on_device(owners, offsets, gradients, embedding, adagrad_state, next_owners, next_offsets):
    devices = lax.axis_size(AXES)
    lookups, columns = gradients.shape
    owned = embedding.shape[0]
    cap = max(2, 4 * lookups // devices)
    rows_out = cap + 2
    blocks = lookups // LANES
    shape = jax.ShapeDtypeStruct
    view = lambda x: x.reshape(blocks, LANES)
    in_hbm = lambda x: pltpu.with_memory_space_constraint(x, pltpu.HBM)

    outgoing, q = pl.pallas_call(
        functools.partial(pack_kernel, cap, rows_out),
        out_shape=(shape((devices * rows_out, columns), BF16), shape((LANES, LANES), I32)),
        in_specs=[ANY] * 5,
        out_specs=(VM, VM),
        scratch_shapes=[pltpu.VMEM((blocks, LANES), I32)] * 4
        + [
            pltpu.VMEM((lookups, columns), BF16),
            pltpu.VMEM((lookups, columns), F32),
            pltpu.VMEM((devices * rows_out, columns), F32),
            pltpu.VMEM((LANES, LANES), I32),
            pltpu.SMEM((LANES, LANES), I32),
            pltpu.SemaphoreType.DMA((6,)),
        ],
        compiler_params=pltpu.CompilerParams(vmem_limit_bytes=12 << 20),
        name="pack",
    )(*map(in_hbm, (view(owners), view(offsets), view(next_owners), view(next_offsets), gradients)))

    def exchange(x, pairs):
        x = x.reshape(devices, pairs, 2, columns)
        x = lax.all_to_all(x, AXES, split_axis=0, concat_axis=0, tiled=True)
        return x.reshape(devices * pairs * 2, columns)

    incoming = exchange(outgoing, rows_out // 2)

    new_embedding, new_state, fetched = pl.pallas_call(
        functools.partial(owner_kernel, cap, rows_out),
        out_shape=(
            shape(embedding.shape, F32),
            shape((owned // LANES, LANES), F32),
            shape((devices * cap, columns), BF16),
        ),
        in_specs=[VM, ANY, ANY],
        out_specs=(ANY, ANY, VM),
        scratch_shapes=[pltpu.VMEM((owned, columns), F32)] * TABLES
        + [
            pltpu.VMEM((devices * rows_out, columns), F32),
            pltpu.VMEM((LANES, devices), I32),
            pltpu.VMEM((LANES, LANES), F32),
            pltpu.VMEM((owned, columns), F32),
            pltpu.VMEM((owned // LANES, LANES), F32),
            pltpu.VMEM((owned // LANES, LANES), F32),
            pltpu.VMEM((owned // LANES, LANES), F32),
            pltpu.SemaphoreType.DMA((4,)),
        ] + [pltpu.SMEM((LANES, devices), I32)],
        compiler_params=pltpu.CompilerParams(vmem_limit_bytes=36 << 20),
        name="owner",
    )(incoming, in_hbm(adagrad_state.reshape(owned // LANES, LANES)), in_hbm(embedding))

    returned = lax.all_to_all(
        fetched.reshape(devices, cap, columns), AXES, split_axis=0, concat_axis=0, tiled=True
    ).reshape(devices * cap, columns)

    next_rows = pl.pallas_call(
        unpack_kernel,
        out_shape=shape((lookups, columns), BF16),
        in_specs=[ANY, VM],
        out_specs=VM,
        scratch_shapes=[
            pltpu.VMEM((devices * cap, columns), F32),
            pltpu.VMEM((lookups, columns), F32),
            pltpu.SMEM((LANES, LANES), I32),
            pltpu.SemaphoreType.DMA,
        ],
        compiler_params=pltpu.CompilerParams(vmem_limit_bytes=12 << 20),
        name="unpack",
    )(q, returned)
    return (new_embedding, new_state.reshape(owned), next_rows)


def solution(mesh):
    line, block = P(AXES), P(AXES, None)
    return jax.shard_map(
        on_device,
        mesh=mesh,
        in_specs=(block, line, block, block, line, block, line),
        out_specs=(block, line, block),
        check_vma=False,
    )
```

```python
import functools

import jax
import jax.numpy as jnp
from jax import lax
from jax.experimental import pallas as pl
from jax.experimental.pallas import tpu as pltpu
from jax.sharding import PartitionSpec as P

AXES = ("dp", "rows")
F32, BF16, I32 = jnp.float32, jnp.bfloat16, jnp.int32
LANES = 128
TABLES = 4


def iota(shape, dim):
    return lax.broadcasted_iota(I32, shape, dim)


def pack_kernel(cap, rows_out, own_hbm, off_hbm, nown_hbm, noff_hbm, g_hbm, out_ref, q_ref,
                own_ref, off_ref, nown_ref, noff_ref, g_ref, gf, outf, pos_v, pos_s, sems):
    loads = [
        pltpu.make_async_copy(src, dst, sems.at[k])
        for k, (src, dst) in enumerate((
            (own_hbm, own_ref), (off_hbm, off_ref), (nown_hbm, nown_ref), (noff_hbm, noff_ref), (g_hbm, g_ref)
        ))
    ]
    for load in loads:
        load.start()
    outf[...] = jnp.zeros_like(outf)
    blocks = own_ref.shape[0]
    devices = out_ref.shape[0] // rows_out
    counts = jnp.concatenate(
        [(iota((LANES, LANES), 0) < iota((LANES, LANES), 1)).astype(BF16), jnp.ones((LANES, LANES), BF16)], axis=1
    )
    row = iota((LANES, LANES), 0)
    meta = jnp.zeros((devices, LANES), F32)

    def slots(o_ref, f_ref, first, meta):
        base = jnp.zeros((devices, LANES), F32)
        out = []
        for b in range(blocks):
            own = o_ref[b:b + 1, :]
            hit = iota((devices, LANES), 0) == own
            hot = hit.astype(BF16)
            count = jnp.dot(hot, counts, preferred_element_type=F32)
            ahead = count[:, 0:LANES] + base
            slot = jnp.sum(jnp.where(hit, ahead, 0.0), axis=0, keepdims=True).astype(I32)
            base = base + count[:, LANES:]
            off = f_ref[b:b + 1, :]
            value = jnp.where(row < first + cap, off // LANES + 1, off % LANES)
            here = (row >= first) & (row < first + 2 * cap) & (row % cap == slot)
            sel = jnp.where(here, value, 0).astype(F32).astype(BF16)
            meta = meta + lax.dot_general(hot, sel, (((1,), (1,)), ((), ())), preferred_element_type=F32)
            out.append((own, slot))
        return out, meta

    loads[0].wait()
    loads[1].wait()
    got, meta = slots(own_ref, off_ref, 0, meta)
    for b, (own, slot) in enumerate(got):
        pos_v[b:b + 1, :] = own * rows_out + slot
    copy = pltpu.make_async_copy(pos_v, pos_s, sems.at[5])
    copy.start()
    for load in loads[2:]:
        load.wait()
    gf[...] = g_ref[...].astype(F32)
    got, meta = slots(nown_ref, noff_ref, 2 * cap, meta)
    for b, (own, slot) in enumerate(got):
        q_ref[b:b + 1, :] = own * cap + slot
    outf[pl.ds(cap, devices, stride=rows_out), :] = meta
    copy.wait()

    def place(b, carry):
        rows = gf.at[pl.ds(pl.multiple_of(b * LANES, LANES), LANES), :]
        for j in range(LANES):
            outf[pl.ds(pos_s[b, j], 1), :] = rows[j:j + 1, :]
        return carry
    lax.fori_loop(0, blocks, place, 0)
    out_ref[...] = outf[...].astype(BF16)


def pick(x, lane):
    return jnp.take_along_axis(x, jnp.full(x.shape, lane, I32), axis=1)


def owner_kernel(cap, rows_in, inc_ref, state_hbm, emb_hbm, nemb_hbm, nstate_hbm, ret_ref,
                 t0, t1, t2, t3, gf, idx_v, cols_v, emb, state_ref, nstate, scales, sems, idx_all):
    devices = idx_v.shape[1]
    owned, columns = emb.shape
    tabs = (t0, t1, t2, t3)
    gf[...] = inc_ref[...].astype(F32)
    m = gf[pl.ds(cap, devices, stride=rows_in), :]
    index = ((m - 1.0) * LANES + pltpu.roll(m, LANES - cap, 1)).astype(I32)
    apart = iota((devices, LANES), 0) * cap + iota((devices, LANES), 1) % cap
    idx_v[...] = jnp.transpose(jnp.where(index < 0, apart % owned, index))
    copies = [
        pltpu.make_async_copy(idx_v.at[pl.ds(2 * cap * k, cap), :], idx_all.at[pl.ds(cap * k, cap), :], sems.at[k + 4])
        for k in range(2)
    ]
    for copy in copies:
        copy.start()
    idx_s = [idx_all.at[i] for i in range(2 * cap)]
    load = pltpu.make_async_copy(emb_hbm, emb, sems.at[0])
    load.start()
    load_state = pltpu.make_async_copy(state_hbm, state_ref, sems.at[3])
    load_state.start()

    def clear(c, carry):
        for t in tabs:
            t[pl.ds(pl.multiple_of(c * 64, 64), 64), :] = jnp.zeros((64, columns), F32)
        return carry
    lax.fori_loop(0, owned // 64, clear, 0)
    copies[0].wait()

    def add(d, carry):
        rows = gf.at[pl.ds(d * rows_in, rows_in), :]
        for i in range(0, cap, TABLES):
            at = [pl.ds(idx_s[i + k][d], 1) for k in range(TABLES)]
            new = [tabs[k][at[k], :] + rows[i + k:i + k + 1, :] for k in range(TABLES)]
            for k in range(TABLES):
                tabs[k][at[k], :] = new[k]
        return carry
    lax.fori_loop(0, devices, add, 0)
    load_state.wait()

    per = 8

    def measure(c, carry):
        means = []
        for k in range(per):
            rows = pl.ds(pl.multiple_of((c * per + k) * LANES, LANES), LANES)
            total = (t0[rows, :] + t1[rows, :]) + (t2[rows, :] + t3[rows, :])
            t0[rows, :] = total
            square = total * total
            high = square.astype(BF16)
            low = (square - high.astype(F32)).astype(BF16)
            both = lax.dot_general(
                jnp.ones((8, 2 * columns), BF16), jnp.concatenate([high, low], axis=1),
                (((1,), (1,)), ((), ())), preferred_element_type=F32,
            )
            means.append(both[0:1, :])
        here = pl.ds(pl.multiple_of(c * per, per), per)
        state = state_ref[here, :] + jnp.concatenate(means, axis=0) * (1.0 / columns)
        nstate[here, :] = state
        scales[here, :] = 0.5 / jnp.sqrt(state)
        return carry
    lax.fori_loop(0, owned // (per * LANES), measure, 0)
    out_state = pltpu.make_async_copy(nstate, nstate_hbm, sems.at[3])
    out_state.start()
    load.wait()

    cols_v[:, 0:owned // LANES] = jnp.transpose(scales[...])
    def update(c, carry):
        for k in range(8):
            rows = pl.ds(pl.multiple_of((c * 8 + k) * LANES, LANES), LANES)
            emb[rows, :] = emb[rows, :] - t0[rows, :] * pick(cols_v[...], c * 8 + k)
        rows = pl.ds(pl.multiple_of(c * 8 * LANES, 8 * LANES), 8 * LANES)
        pltpu.make_async_copy(emb.at[rows, :], nemb_hbm.at[rows, :], sems.at[2]).start()
        return carry
    lax.fori_loop(0, owned // (8 * LANES), update, 0)

    copies[1].wait()

    def fetch(d, carry):
        rows = gf.at[pl.ds(pl.multiple_of(d * cap, cap), cap), :]
        for i in range(cap):
            rows[i:i + 1, :] = emb[pl.ds(idx_s[cap + i][d], 1), :]
        return carry
    lax.fori_loop(0, devices, fetch, 0)
    ret_ref[...] = gf[0:devices * cap, :].astype(BF16)
    out_state.wait()
    pltpu.make_async_copy(emb, nemb_hbm, sems.at[2]).wait()


def unpack_kernel(q_any, ret_ref, out_hbm, wide, rows, out_ref, q_ref, sems):
    copy = pltpu.make_async_copy(q_any, q_ref, sems.at[0])
    copy.start()
    wide[...] = ret_ref[...].astype(F32)
    copy.wait()

    def take(b, carry):
        here = rows.at[pl.ds(pl.multiple_of(b * LANES, LANES), LANES), :]
        for j in range(LANES):
            here[j:j + 1, :] = wide[pl.ds(q_ref[b, j], 1), :]
        block = pl.ds(pl.multiple_of(b * LANES, LANES), LANES)
        out_ref[block, :] = here[...].astype(BF16)
        pltpu.make_async_copy(out_ref.at[block, :], out_hbm.at[block, :], sems.at[1]).start()
        return carry
    lax.fori_loop(0, out_ref.shape[0] // LANES, take, 0)
    pltpu.make_async_copy(out_ref, out_hbm, sems.at[1]).wait()


VM = pl.BlockSpec(memory_space=pltpu.VMEM)
ANY = pl.BlockSpec(memory_space=pl.ANY)


def on_device(owners, offsets, gradients, embedding, adagrad_state, next_owners, next_offsets):
    devices = lax.axis_size(AXES)
    lookups, columns = gradients.shape
    owned = embedding.shape[0]
    cap = max(2, 4 * lookups // devices)
    rows_out = cap + 2
    blocks = lookups // LANES
    shape = jax.ShapeDtypeStruct
    view = lambda x: x.reshape(blocks, LANES)
    in_hbm = lambda x: pltpu.with_memory_space_constraint(x, pltpu.HBM)

    outgoing, q = pl.pallas_call(
        functools.partial(pack_kernel, cap, rows_out),
        out_shape=(shape((devices * rows_out, columns), BF16), shape((blocks, LANES), I32)),
        in_specs=[ANY] * 5,
        out_specs=(VM, VM),
        scratch_shapes=[pltpu.VMEM((blocks, LANES), I32)] * 4
        + [
            pltpu.VMEM((lookups, columns), BF16),
            pltpu.VMEM((lookups, columns), F32),
            pltpu.VMEM((devices * rows_out, columns), F32),
            pltpu.VMEM((blocks, LANES), I32),
            pltpu.SMEM((blocks, LANES), I32),
            pltpu.SemaphoreType.DMA((6,)),
        ],
        compiler_params=pltpu.CompilerParams(vmem_limit_bytes=12 << 20),
        name="pack",
    )(*map(in_hbm, (view(owners), view(offsets), view(next_owners), view(next_offsets), gradients)))

    def exchange(x, pairs):
        x = x.reshape(devices, pairs, 2, columns)
        x = lax.all_to_all(x, AXES, split_axis=0, concat_axis=0, tiled=True)
        return x.reshape(devices * pairs * 2, columns)

    incoming = exchange(outgoing, rows_out // 2)

    new_embedding, new_state, fetched = pl.pallas_call(
        functools.partial(owner_kernel, cap, rows_out),
        out_shape=(
            shape(embedding.shape, F32),
            shape((owned // LANES, LANES), F32),
            shape((devices * cap, columns), BF16),
        ),
        in_specs=[VM, ANY, ANY],
        out_specs=(ANY, ANY, VM),
        scratch_shapes=[pltpu.VMEM((owned, columns), F32)] * TABLES
        + [
            pltpu.VMEM((devices * rows_out, columns), F32),
            pltpu.VMEM((LANES, devices), I32),
            pltpu.VMEM((LANES, LANES), F32),
            pltpu.VMEM((owned, columns), F32),
            pltpu.VMEM((owned // LANES, LANES), F32),
            pltpu.VMEM((owned // LANES, LANES), F32),
            pltpu.VMEM((owned // LANES, LANES), F32),
            pltpu.SemaphoreType.DMA((6,)),
            pltpu.SMEM((2 * cap, devices), I32),
        ],
        compiler_params=pltpu.CompilerParams(vmem_limit_bytes=36 << 20),
        name="owner",
    )(incoming, in_hbm(adagrad_state.reshape(owned // LANES, LANES)), in_hbm(embedding))

    returned = lax.all_to_all(
        fetched.reshape(devices, cap, columns), AXES, split_axis=0, concat_axis=0, tiled=True
    ).reshape(devices * cap, columns)

    next_rows = pl.pallas_call(
        unpack_kernel,
        out_shape=shape((lookups, columns), BF16),
        in_specs=[ANY, VM],
        out_specs=ANY,
        scratch_shapes=[
            pltpu.VMEM((devices * cap, columns), F32),
            pltpu.VMEM((lookups, columns), F32),
            pltpu.VMEM((lookups, columns), BF16),
            pltpu.SMEM((blocks, LANES), I32),
            pltpu.SemaphoreType.DMA((2,)),
        ],
        compiler_params=pltpu.CompilerParams(vmem_limit_bytes=12 << 20),
        name="unpack",
    )(q, returned)
    return (new_embedding, new_state.reshape(owned), next_rows)


def solution(mesh):
    line, block = P(AXES), P(AXES, None)
    return jax.shard_map(
        on_device,
        mesh=mesh,
        in_specs=(block, line, block, block, line, block, line),
        out_specs=(block, line, block),
        check_vma=False,
    )
```

```python
import functools

import jax
import jax.numpy as jnp
from jax import lax
from jax.experimental import pallas as pl
from jax.experimental.pallas import tpu as pltpu
from jax.sharding import PartitionSpec as P

AXES = ("dp", "rows")
F32, BF16, I32 = jnp.float32, jnp.bfloat16, jnp.int32
LANES = 128
TABLES = 4


def iota(shape, dim):
    return lax.broadcasted_iota(I32, shape, dim)


def pack_kernel(cap, rows_out, own_hbm, off_hbm, nown_hbm, noff_hbm, g_hbm, out_ref, q_ref,
                t0, t1, t2, t3, own_ref, off_ref, nown_ref, noff_ref, g_ref, gf, outf, pos_v, pos_s, sems):
    blocks = own_ref.shape[0]
    devices = out_ref.shape[0] // rows_out
    loads = [
        pltpu.make_async_copy(src, dst, sems.at[k])
        for k, (src, dst) in enumerate((
            (own_hbm, own_ref), (off_hbm, off_ref), (nown_hbm, nown_ref), (noff_hbm, noff_ref), (g_hbm, g_ref)
        ))
    ]
    for load in loads:
        load.start()
    outf[...] = jnp.zeros_like(outf)

    def clear(tabs):
        def step(c, carry):
            for t in tabs:
                t[pl.ds(pl.multiple_of(c * 128, 128), 128), :] = jnp.zeros((128, t.shape[1]), F32)
            return carry
        lax.fori_loop(0, t0.shape[0] // 128, step, 0)

    clear((t0, t1))
    counts = jnp.concatenate(
        [(iota((LANES, LANES), 0) < iota((LANES, LANES), 1)).astype(BF16), jnp.ones((LANES, LANES), BF16)], axis=1
    )
    row = iota((cap, LANES), 0)
    bases = [jnp.zeros((devices, LANES), F32)] * 2
    metas = [jnp.zeros((devices, 2 * cap), F32)] * 2
    for load in loads[:4]:
        load.wait()
    for b in range(blocks):
        for n, (o_ref, f_ref) in enumerate(((own_ref, off_ref), (nown_ref, noff_ref))):
            own, off = o_ref[b:b + 1, :], f_ref[b:b + 1, :]
            hit = jnp.where(iota((devices, LANES), 0) == own, 1.0, 0.0)
            hot = hit.astype(BF16)
            count = jnp.dot(hot, counts, preferred_element_type=F32)
            ahead = count[:, 0:LANES] + bases[n]
            slot = jnp.sum(hit * ahead, axis=0, keepdims=True).astype(I32)
            bases[n] = bases[n] + count[:, LANES:]
            values = (off // LANES + 1, off % LANES)
            sel = jnp.concatenate(
                [jnp.where(row == slot, value.astype(F32), 0.0) for value in values], axis=0
            ).astype(BF16)
            metas[n] = metas[n] + lax.dot_general(
                hot, sel, (((1,), (1,)), ((), ())), preferred_element_type=F32
            )
            if n == 0:
                pos_v[b:b + 1, :] = own * rows_out + slot
            else:
                q_ref[b:b + 1, :] = own * cap + slot
    copy = pltpu.make_async_copy(pos_v, pos_s, sems.at[5])
    copy.start()
    outf[pl.ds(cap, devices, stride=rows_out), :] = jnp.concatenate(metas, axis=1)
    loads[4].wait()
    gf[...] = g_ref[...].astype(F32)
    clear((t2, t3))
    copy.wait()

    def place(b, carry):
        rows = gf.at[pl.ds(pl.multiple_of(b * LANES, LANES), LANES), :]
        for j in range(LANES):
            outf[pl.ds(pos_s[b, j], 1), :] = rows[j:j + 1, :]
        return carry
    lax.fori_loop(0, blocks, place, 0)
    out_ref[...] = outf[...].astype(BF16)


def pick(x, lane):
    return jnp.take_along_axis(x, jnp.full(x.shape, lane, I32), axis=1)


def owner_kernel(cap, rows_in, inc_ref, state_hbm, emb_hbm, _0, _1, _2, _3, nemb_hbm, nstate_hbm, ret_ref,
                 t0, t1, t2, t3, gf, idx_v, cols_v, emb, state_ref, nstate, scales, sems, idx_all):
    devices = idx_v.shape[1]
    owned, columns = emb.shape
    tabs = (t0, t1, t2, t3)
    gf[...] = inc_ref[...].astype(F32)
    m = gf[pl.ds(cap, devices, stride=rows_in), :]
    index = ((m - 1.0) * LANES + pltpu.roll(m, LANES - cap, 1)).astype(I32)
    apart = iota((devices, LANES), 0) * cap + iota((devices, LANES), 1) % cap
    idx_v[...] = jnp.transpose(jnp.where(index < 0, apart % owned, index))
    copies = [
        pltpu.make_async_copy(idx_v.at[pl.ds(2 * cap * k, cap), :], idx_all.at[pl.ds(cap * k, cap), :], sems.at[k + 4])
        for k in range(2)
    ]
    for copy in copies:
        copy.start()
    idx_s = [idx_all.at[i] for i in range(2 * cap)]
    load = pltpu.make_async_copy(emb_hbm, emb, sems.at[0])
    load.start()
    load_state = pltpu.make_async_copy(state_hbm, state_ref, sems.at[3])
    load_state.start()

    copies[0].wait()

    def add(d, carry):
        rows = gf.at[pl.ds(d * rows_in, rows_in), :]
        for i in range(0, cap, TABLES):
            at = [pl.ds(idx_s[i + k][d], 1) for k in range(TABLES)]
            new = [tabs[k][at[k], :] + rows[i + k:i + k + 1, :] for k in range(TABLES)]
            for k in range(TABLES):
                tabs[k][at[k], :] = new[k]
        return carry
    lax.fori_loop(0, devices, add, 0)
    load_state.wait()

    per = 8

    def measure(c, carry):
        means = []
        for k in range(per):
            rows = pl.ds(pl.multiple_of((c * per + k) * LANES, LANES), LANES)
            total = (t0[rows, :] + t1[rows, :]) + (t2[rows, :] + t3[rows, :])
            t0[rows, :] = total
            square = total * total
            high = square.astype(BF16)
            low = (square - high.astype(F32)).astype(BF16)
            both = lax.dot_general(
                jnp.ones((8, 2 * columns), BF16), jnp.concatenate([high, low], axis=1),
                (((1,), (1,)), ((), ())), preferred_element_type=F32,
            )
            means.append(both[0:1, :])
        here = pl.ds(pl.multiple_of(c * per, per), per)
        state = state_ref[here, :] + jnp.concatenate(means, axis=0) * (1.0 / columns)
        nstate[here, :] = state
        scales[here, :] = 0.5 / jnp.sqrt(state)
        return carry
    lax.fori_loop(0, owned // (per * LANES), measure, 0)
    out_state = pltpu.make_async_copy(nstate, nstate_hbm, sems.at[3])
    out_state.start()
    load.wait()

    cols_v[:, 0:owned // LANES] = jnp.transpose(scales[...])
    def update(c, carry):
        for k in range(8):
            rows = pl.ds(pl.multiple_of((c * 8 + k) * LANES, LANES), LANES)
            emb[rows, :] = emb[rows, :] - t0[rows, :] * pick(cols_v[...], c * 8 + k)
        rows = pl.ds(pl.multiple_of(c * 8 * LANES, 8 * LANES), 8 * LANES)
        pltpu.make_async_copy(emb.at[rows, :], nemb_hbm.at[rows, :], sems.at[2]).start()
        return carry
    lax.fori_loop(0, owned // (8 * LANES), update, 0)

    copies[1].wait()

    def narrow(d):
        rows = pl.ds(pl.multiple_of(d * cap, cap), cap)
        ret_ref[rows, :] = gf[rows, :].astype(BF16)

    def fetch(d, carry):
        rows = gf.at[pl.ds(pl.multiple_of(d * cap, cap), cap), :]
        for i in range(cap):
            rows[i:i + 1, :] = emb[pl.ds(idx_s[cap + i][d], 1), :]
        narrow(jnp.maximum(d - 1, 0))
        return carry
    lax.fori_loop(0, devices, fetch, 0)
    narrow(devices - 1)
    out_state.wait()
    pltpu.make_async_copy(emb, nemb_hbm, sems.at[2]).wait()


def unpack_kernel(q_any, ret_ref, out_hbm, wide, rows, out_ref, q_ref, sems):
    copy = pltpu.make_async_copy(q_any, q_ref, sems.at[0])
    copy.start()
    wide[...] = ret_ref[...].astype(F32)
    copy.wait()

    def take(b, carry):
        here = rows.at[pl.ds(pl.multiple_of(b * LANES, LANES), LANES), :]
        for j in range(LANES):
            here[j:j + 1, :] = wide[pl.ds(q_ref[b, j], 1), :]
        block = pl.ds(pl.multiple_of(b * LANES, LANES), LANES)
        out_ref[block, :] = here[...].astype(BF16)
        pltpu.make_async_copy(out_ref.at[block, :], out_hbm.at[block, :], sems.at[1]).start()
        return carry
    lax.fori_loop(0, out_ref.shape[0] // LANES, take, 0)
    pltpu.make_async_copy(out_ref, out_hbm, sems.at[1]).wait()


VM = pl.BlockSpec(memory_space=pltpu.VMEM)
ANY = pl.BlockSpec(memory_space=pl.ANY)


def on_device(owners, offsets, gradients, embedding, adagrad_state, next_owners, next_offsets):
    devices = lax.axis_size(AXES)
    lookups, columns = gradients.shape
    owned = embedding.shape[0]
    cap = max(2, 4 * lookups // devices)
    rows_out = cap + 2
    blocks = lookups // LANES
    shape = jax.ShapeDtypeStruct
    view = lambda x: x.reshape(blocks, LANES)
    in_hbm = lambda x: pltpu.with_memory_space_constraint(x, pltpu.HBM)

    table = pltpu.VMEM((owned, columns), F32)
    outgoing, q, *tables = pl.pallas_call(
        functools.partial(pack_kernel, cap, rows_out),
        out_shape=(shape((devices * rows_out, columns), BF16), shape((blocks, LANES), I32))
        + (table,) * TABLES,
        in_specs=[ANY] * 5,
        out_specs=(VM,) * (2 + TABLES),
        scratch_shapes=[pltpu.VMEM((blocks, LANES), I32)] * 4
        + [
            pltpu.VMEM((lookups, columns), BF16),
            pltpu.VMEM((lookups, columns), F32),
            pltpu.VMEM((devices * rows_out, columns), F32),
            pltpu.VMEM((blocks, LANES), I32),
            pltpu.SMEM((blocks, LANES), I32),
            pltpu.SemaphoreType.DMA((6,)),
        ],
        compiler_params=pltpu.CompilerParams(vmem_limit_bytes=12 << 20),
        name="pack",
    )(*map(in_hbm, (view(owners), view(offsets), view(next_owners), view(next_offsets), gradients)))

    def exchange(x, pairs):
        x = x.reshape(devices, pairs, 2, columns)
        x = lax.all_to_all(x, AXES, split_axis=0, concat_axis=0, tiled=True)
        return x.reshape(devices * pairs * 2, columns)

    incoming = exchange(outgoing, rows_out // 2)

    new_embedding, new_state, fetched = pl.pallas_call(
        functools.partial(owner_kernel, cap, rows_out),
        out_shape=(
            shape(embedding.shape, F32),
            shape((owned // LANES, LANES), F32),
            shape((devices * cap, columns), BF16),
        ) + (table,) * TABLES,
        in_specs=[VM, ANY, ANY] + [VM] * TABLES,
        out_specs=(ANY, ANY, VM) + (VM,) * TABLES,
        scratch_shapes=[
            pltpu.VMEM((devices * rows_out, columns), F32),
            pltpu.VMEM((LANES, devices), I32),
            pltpu.VMEM((LANES, LANES), F32),
            pltpu.VMEM((owned, columns), F32),
            pltpu.VMEM((owned // LANES, LANES), F32),
            pltpu.VMEM((owned // LANES, LANES), F32),
            pltpu.VMEM((owned // LANES, LANES), F32),
            pltpu.SemaphoreType.DMA((6,)),
            pltpu.SMEM((2 * cap, devices), I32),
        ],
        input_output_aliases={3 + k: 3 + k for k in range(TABLES)},
        compiler_params=pltpu.CompilerParams(vmem_limit_bytes=16 << 20),
        name="owner",
    )(incoming, in_hbm(adagrad_state.reshape(owned // LANES, LANES)), in_hbm(embedding),
      *[pltpu.with_memory_space_constraint(t, pltpu.VMEM) for t in tables])[:3]

    returned = lax.all_to_all(
        fetched.reshape(devices, cap, columns), AXES, split_axis=0, concat_axis=0, tiled=True
    ).reshape(devices * cap, columns)

    next_rows = pl.pallas_call(
        unpack_kernel,
        out_shape=shape((lookups, columns), BF16),
        in_specs=[ANY, VM],
        out_specs=ANY,
        scratch_shapes=[
            pltpu.VMEM((devices * cap, columns), F32),
            pltpu.VMEM((lookups, columns), F32),
            pltpu.VMEM((lookups, columns), BF16),
            pltpu.SMEM((blocks, LANES), I32),
            pltpu.SemaphoreType.DMA((2,)),
        ],
        compiler_params=pltpu.CompilerParams(vmem_limit_bytes=12 << 20),
        name="unpack",
    )(q, returned)
    return (new_embedding, new_state.reshape(owned), next_rows)


def solution(mesh):
    line, block = P(AXES), P(AXES, None)
    return jax.shard_map(
        on_device,
        mesh=mesh,
        in_specs=(block, line, block, block, line, block, line),
        out_specs=(block, line, block),
        check_vma=False,
    )
```

```python
import functools

import jax
import jax.numpy as jnp
from jax import lax
from jax.experimental import pallas as pl
from jax.experimental.pallas import tpu as pltpu
from jax.sharding import PartitionSpec as P

AXES = ("dp", "rows")
F32, BF16, I32 = jnp.float32, jnp.bfloat16, jnp.int32
LANES = 128
TABLES = 4


def iota(shape, dim):
    return lax.broadcasted_iota(I32, shape, dim)


def pack_kernel(cap, rows_out, own_hbm, off_hbm, nown_hbm, noff_hbm, g_hbm, out_ref, q_ref,
                own_ref, off_ref, nown_ref, noff_ref, g_ref, gf, outf, pos_v, pos_s, sems):
    loads = [
        pltpu.make_async_copy(src, dst, sems.at[k])
        for k, (src, dst) in enumerate((
            (own_hbm, own_ref), (off_hbm, off_ref), (nown_hbm, nown_ref), (noff_hbm, noff_ref), (g_hbm, g_ref)
        ))
    ]
    for load in loads:
        load.start()
    outf[...] = jnp.zeros_like(outf)
    blocks = own_ref.shape[0]
    devices = out_ref.shape[0] // rows_out
    counts = jnp.concatenate(
        [(iota((LANES, LANES), 0) < iota((LANES, LANES), 1)).astype(BF16), jnp.ones((LANES, LANES), BF16)], axis=1
    )
    row = iota((2 * cap, LANES), 0)
    name = iota((devices, LANES), 0).astype(F32).astype(BF16)

    def slots(o_ref, f_ref):
        base = jnp.zeros((devices, LANES), F32)
        out, hots, sels = [], [], []
        for b in range(blocks):
            own = o_ref[b:b + 1, :]
            hot = jnp.where(name == own.astype(F32).astype(BF16), jnp.bfloat16(1), jnp.bfloat16(0))
            count = jnp.dot(hot, counts, preferred_element_type=F32)
            ahead = (count[:, 0:LANES] + base).astype(BF16)
            slot = jnp.sum((hot * ahead).astype(F32), axis=0, keepdims=True).astype(I32)
            base = base + count[:, LANES:]
            off = f_ref[b:b + 1, :]
            value = jnp.where(row < cap, off // LANES + 1, off % LANES)
            sel = jnp.where(row % cap == slot, value, 0).astype(F32).astype(BF16)
            hots.append(hot)
            sels.append(sel)
            out.append((own, slot))
        meta = lax.dot_general(
            jnp.concatenate(hots, axis=1), jnp.concatenate(sels, axis=1), (((1,), (1,)), ((), ())),
            preferred_element_type=F32,
        )
        return out, meta

    loads[0].wait()
    loads[1].wait()
    got, sent = slots(own_ref, off_ref)
    for b, (own, slot) in enumerate(got):
        pos_v[b:b + 1, :] = own * rows_out + slot
    copy = pltpu.make_async_copy(pos_v, pos_s, sems.at[5])
    copy.start()
    for load in loads[2:]:
        load.wait()
    gf[...] = g_ref[...].astype(F32)
    got, asked = slots(nown_ref, noff_ref)
    for b, (own, slot) in enumerate(got):
        q_ref[b:b + 1, :] = own * cap + slot
    outf[pl.ds(cap, devices, stride=rows_out), :] = jnp.concatenate([sent, asked], axis=1)
    copy.wait()

    def place(i, carry):
        for u in range(16):
            for b in range(blocks):
                outf[pl.ds(pos_s.at[b][i * 16 + u], 1), :] = gf[pl.ds(b * LANES + i * 16 + u, 1), :]
        return carry
    lax.fori_loop(0, LANES // 16, place, 0)
    out_ref[...] = outf[...].astype(BF16)


def pick(x, lane):
    return jnp.take_along_axis(x, jnp.full(x.shape, lane, I32), axis=1)


def owner_kernel(cap, rows_in, inc_ref, state_hbm, emb_hbm, nemb_hbm, nstate_hbm, ret_ref,
                 t0, t1, t2, t3, gf, idx_v, cols_v, emb, state_ref, nstate, scales, sems, idx_all):
    devices = idx_v.shape[1]
    owned, columns = emb.shape
    tabs = (t0, t1, t2, t3)
    gf[...] = inc_ref[...].astype(F32)
    m = gf[pl.ds(cap, devices, stride=rows_in), :]
    index = ((m - 1.0) * LANES + pltpu.roll(m, LANES - cap, 1)).astype(I32)
    apart = iota((devices, LANES), 0) * cap + iota((devices, LANES), 1) % cap
    idx_v[...] = jnp.transpose(jnp.where(index < 0, apart % owned, index))
    copies = [
        pltpu.make_async_copy(idx_v.at[pl.ds(2 * cap * k, cap), :], idx_all.at[pl.ds(cap * k, cap), :], sems.at[k + 4])
        for k in range(2)
    ]
    for copy in copies:
        copy.start()
    idx_s = [idx_all.at[i] for i in range(2 * cap)]
    load = pltpu.make_async_copy(emb_hbm, emb, sems.at[0])
    load.start()
    load_state = pltpu.make_async_copy(state_hbm, state_ref, sems.at[3])
    load_state.start()

    def clear(c, carry):
        for t in tabs:
            t[pl.ds(pl.multiple_of(c * 64, 64), 64), :] = jnp.zeros((64, columns), F32)
        return carry
    lax.fori_loop(0, owned // 64, clear, 0)
    copies[0].wait()

    def add(c, carry):
        for n in range(8):
            d = c * 8 + n
            rows = gf.at[pl.ds(d * rows_in, rows_in), :]
            for i in range(0, cap, TABLES):
                at = [pl.ds(idx_s[i + k][d], 1) for k in range(TABLES)]
                new = [tabs[k][at[k], :] + rows[i + k:i + k + 1, :] for k in range(TABLES)]
                for k in range(TABLES):
                    tabs[k][at[k], :] = new[k]
        return carry
    lax.fori_loop(0, devices // 8, add, 0)
    load_state.wait()

    per = 8

    def measure(c, carry):
        means = []
        for k in range(per):
            rows = pl.ds(pl.multiple_of((c * per + k) * LANES, LANES), LANES)
            total = (t0[rows, :] + t1[rows, :]) + (t2[rows, :] + t3[rows, :])
            t0[rows, :] = total
            square = total * total
            high = square.astype(BF16)
            low = (square - high.astype(F32)).astype(BF16)
            both = lax.dot_general(
                jnp.ones((8, 2 * columns), BF16), jnp.concatenate([high, low], axis=1),
                (((1,), (1,)), ((), ())), preferred_element_type=F32,
            )
            means.append(both[0:1, :])
        here = pl.ds(pl.multiple_of(c * per, per), per)
        state = state_ref[here, :] + jnp.concatenate(means, axis=0) * (1.0 / columns)
        nstate[here, :] = state
        scales[here, :] = 0.5 / jnp.sqrt(state)
        return carry
    lax.fori_loop(0, owned // (per * LANES), measure, 0)
    out_state = pltpu.make_async_copy(nstate, nstate_hbm, sems.at[3])
    out_state.start()
    load.wait()

    cols_v[:, 0:owned // LANES] = jnp.transpose(scales[...])
    def update(c, carry):
        for k in range(8):
            rows = pl.ds(pl.multiple_of((c * 8 + k) * LANES, LANES), LANES)
            emb[rows, :] = emb[rows, :] - t0[rows, :] * pick(cols_v[...], c * 8 + k)
        rows = pl.ds(pl.multiple_of(c * 8 * LANES, 8 * LANES), 8 * LANES)
        pltpu.make_async_copy(emb.at[rows, :], nemb_hbm.at[rows, :], sems.at[2]).start()
        return carry
    lax.fori_loop(0, owned // (8 * LANES), update, 0)

    copies[1].wait()

    def fetch(c, carry):
        for n in range(8):
            d = c * 8 + n
            rows = gf.at[pl.ds(pl.multiple_of(d * cap, cap), cap), :]
            for i in range(cap):
                rows[i:i + 1, :] = emb[pl.ds(idx_s[cap + i][d], 1), :]
        return carry
    lax.fori_loop(0, devices // 8, fetch, 0)
    ret_ref[...] = gf[0:devices * cap, :].astype(BF16)
    out_state.wait()
    pltpu.make_async_copy(emb, nemb_hbm, sems.at[2]).wait()


def unpack_kernel(q_any, ret_ref, out_ref, wide, rows, q_ref, sem):
    copy = pltpu.make_async_copy(q_any, q_ref, sem)
    copy.start()
    wide[...] = ret_ref[...].astype(F32)
    copy.wait()

    def take(i, carry):
        for u in range(16):
            for b in range(q_ref.shape[0]):
                rows[pl.ds(b * LANES + i * 16 + u, 1), :] = wide[pl.ds(q_ref.at[b][i * 16 + u], 1), :]
        return carry
    lax.fori_loop(0, LANES // 16, take, 0)
    out_ref[...] = rows[...].astype(BF16)


VM = pl.BlockSpec(memory_space=pltpu.VMEM)
ANY = pl.BlockSpec(memory_space=pl.ANY)


def on_device(owners, offsets, gradients, embedding, adagrad_state, next_owners, next_offsets):
    devices = lax.axis_size(AXES)
    lookups, columns = gradients.shape
    owned = embedding.shape[0]
    cap = max(2, 4 * lookups // devices)
    rows_out = cap + 2
    blocks = lookups // LANES
    shape = jax.ShapeDtypeStruct
    view = lambda x: x.reshape(blocks, LANES)
    in_hbm = lambda x: pltpu.with_memory_space_constraint(x, pltpu.HBM)

    outgoing, q = pl.pallas_call(
        functools.partial(pack_kernel, cap, rows_out),
        out_shape=(shape((devices * rows_out, columns), BF16), shape((blocks, LANES), I32)),
        in_specs=[ANY] * 5,
        out_specs=(VM, VM),
        scratch_shapes=[pltpu.VMEM((blocks, LANES), I32)] * 4
        + [
            pltpu.VMEM((lookups, columns), BF16),
            pltpu.VMEM((lookups, columns), F32),
            pltpu.VMEM((devices * rows_out, columns), F32),
            pltpu.VMEM((blocks, LANES), I32),
            pltpu.SMEM((blocks, LANES), I32),
            pltpu.SemaphoreType.DMA((6,)),
        ],
        compiler_params=pltpu.CompilerParams(vmem_limit_bytes=12 << 20),
        name="pack",
    )(*map(in_hbm, (view(owners), view(offsets), view(next_owners), view(next_offsets), gradients)))

    def exchange(x, pairs):
        x = x.reshape(devices, pairs, 2, columns)
        x = lax.all_to_all(x, AXES, split_axis=0, concat_axis=0, tiled=True)
        return x.reshape(devices * pairs * 2, columns)

    incoming = exchange(outgoing, rows_out // 2)

    new_embedding, new_state, fetched = pl.pallas_call(
        functools.partial(owner_kernel, cap, rows_out),
        out_shape=(
            shape(embedding.shape, F32),
            shape((owned // LANES, LANES), F32),
            shape((devices * cap, columns), BF16),
        ),
        in_specs=[VM, ANY, ANY],
        out_specs=(ANY, ANY, VM),
        scratch_shapes=[pltpu.VMEM((owned, columns), F32)] * TABLES
        + [
            pltpu.VMEM((devices * rows_out, columns), F32),
            pltpu.VMEM((LANES, devices), I32),
            pltpu.VMEM((LANES, LANES), F32),
            pltpu.VMEM((owned, columns), F32),
            pltpu.VMEM((owned // LANES, LANES), F32),
            pltpu.VMEM((owned // LANES, LANES), F32),
            pltpu.VMEM((owned // LANES, LANES), F32),
            pltpu.SemaphoreType.DMA((6,)),
            pltpu.SMEM((2 * cap, devices), I32),
        ],
        compiler_params=pltpu.CompilerParams(vmem_limit_bytes=36 << 20),
        name="owner",
    )(incoming, in_hbm(adagrad_state.reshape(owned // LANES, LANES)), in_hbm(embedding))

    returned = lax.all_to_all(
        fetched.reshape(devices, cap, columns), AXES, split_axis=0, concat_axis=0, tiled=True
    ).reshape(devices * cap, columns)

    next_rows = pl.pallas_call(
        unpack_kernel,
        out_shape=shape((lookups, columns), BF16),
        in_specs=[ANY, VM],
        out_specs=VM,
        scratch_shapes=[
            pltpu.VMEM((devices * cap, columns), F32),
            pltpu.VMEM((lookups, columns), F32),
            pltpu.SMEM((blocks, LANES), I32),
            pltpu.SemaphoreType.DMA,
        ],
        compiler_params=pltpu.CompilerParams(vmem_limit_bytes=12 << 20),
        name="unpack",
    )(q, returned)
    return (new_embedding, new_state.reshape(owned), next_rows)


def solution(mesh):
    line, block = P(AXES), P(AXES, None)
    return jax.shard_map(
        on_device,
        mesh=mesh,
        in_specs=(block, line, block, block, line, block, line),
        out_specs=(block, line, block),
        check_vma=False,
    )
```

```python
import functools

import jax
import jax.numpy as jnp
from jax import lax
from jax.experimental import pallas as pl
from jax.experimental.pallas import tpu as pltpu
from jax.sharding import PartitionSpec as P

AXES = ("dp", "rows")
F32, BF16, I32 = jnp.float32, jnp.bfloat16, jnp.int32
LANES = 128
TABLES = 4


def iota(shape, dim):
    return lax.broadcasted_iota(I32, shape, dim)


def pack_kernel(cap, rows_out, own_hbm, off_hbm, nown_hbm, noff_hbm, g_hbm, out_ref, q_ref,
                own_ref, off_ref, nown_ref, noff_ref, g_ref, gf, outf, pos_v, pos_s, sems):
    loads = [
        pltpu.make_async_copy(src, dst, sems.at[k])
        for k, (src, dst) in enumerate((
            (own_hbm, own_ref), (off_hbm, off_ref), (nown_hbm, nown_ref), (noff_hbm, noff_ref), (g_hbm, g_ref)
        ))
    ]
    for load in loads:
        load.start()
    outf[...] = jnp.zeros_like(outf)
    blocks = own_ref.shape[0]
    devices = out_ref.shape[0] // rows_out
    counts = jnp.concatenate(
        [(iota((LANES, LANES), 0) < iota((LANES, LANES), 1)).astype(BF16), jnp.ones((LANES, LANES), BF16)], axis=1
    )
    row = iota((2 * cap, LANES), 0)
    name = iota((devices, LANES), 0).astype(F32).astype(BF16)

    def slots(o_ref, f_ref):
        base = jnp.zeros((devices, LANES), F32)
        out, hots, sels = [], [], []
        for b in range(blocks):
            own = o_ref[b:b + 1, :]
            hot = jnp.where(name == own.astype(F32).astype(BF16), jnp.bfloat16(1), jnp.bfloat16(0))
            count = jnp.dot(hot, counts, preferred_element_type=F32)
            ahead = (count[:, 0:LANES] + base).astype(BF16)
            slot = jnp.sum((hot * ahead).astype(F32), axis=0, keepdims=True).astype(I32)
            base = base + count[:, LANES:]
            off = f_ref[b:b + 1, :]
            value = jnp.where(row < cap, off // LANES + 1, off % LANES)
            sel = jnp.where(row % cap == slot, value, 0).astype(F32).astype(BF16)
            hots.append(hot)
            sels.append(sel)
            out.append((own, slot))
        meta = lax.dot_general(
            jnp.concatenate(hots, axis=1), jnp.concatenate(sels, axis=1), (((1,), (1,)), ((), ())),
            preferred_element_type=F32,
        )
        return out, meta

    loads[0].wait()
    loads[1].wait()
    got, sent = slots(own_ref, off_ref)
    for b, (own, slot) in enumerate(got):
        pos_v[b:b + 1, :] = own * rows_out + slot
    copy = pltpu.make_async_copy(pos_v, pos_s, sems.at[5])
    copy.start()
    for load in loads[2:]:
        load.wait()
    gf[...] = g_ref[...].astype(F32)
    got, asked = slots(nown_ref, noff_ref)
    for b, (own, slot) in enumerate(got):
        q_ref[b:b + 1, :] = own * cap + slot
    outf[pl.ds(cap, devices, stride=rows_out), :] = jnp.concatenate([sent, asked], axis=1)
    copy.wait()

    def place(i, carry):
        for u in range(16):
            for b in range(blocks):
                outf[pl.ds(pos_s.at[b][i * 16 + u], 1), :] = gf[pl.ds(b * LANES + i * 16 + u, 1), :]
        return carry
    lax.fori_loop(0, LANES // 16, place, 0)
    out_ref[...] = outf[...].astype(BF16)


def pick(x, lane):
    return jnp.take_along_axis(x, jnp.full(x.shape, lane, I32), axis=1)


def owner_kernel(cap, rows_in, inc_ref, state_hbm, emb_hbm, nemb_hbm, nstate_hbm, ret_ref,
                 gf, idx_v, cols_v, emb, state_ref, nstate, scales, sems, idx_all, *tabs):
    devices = idx_v.shape[1]
    owned, columns = emb.shape
    gf[...] = inc_ref[...].astype(F32)
    m = gf[pl.ds(cap, devices, stride=rows_in), :]
    index = ((m - 1.0) * LANES + pltpu.roll(m, LANES - cap, 1)).astype(I32)
    apart = iota((devices, LANES), 0) * cap + iota((devices, LANES), 1) % cap
    idx_v[...] = jnp.transpose(jnp.where(index < 0, apart % owned, index))
    copies = [
        pltpu.make_async_copy(idx_v.at[pl.ds(2 * cap * k, cap), :], idx_all.at[pl.ds(cap * k, cap), :], sems.at[k + 4])
        for k in range(2)
    ]
    for copy in copies:
        copy.start()
    idx_s = [idx_all.at[i] for i in range(2 * cap)]
    load = pltpu.make_async_copy(emb_hbm, emb, sems.at[0])
    load.start()
    load_state = pltpu.make_async_copy(state_hbm, state_ref, sems.at[3])
    load_state.start()

    def clear(c, carry):
        for t in tabs:
            t[pl.ds(pl.multiple_of(c * 256, 256), 256), :] = jnp.zeros((256, columns), F32)
        return carry
    lax.fori_loop(0, owned // 256, clear, 0)
    copies[0].wait()

    def add(c, carry):
        for n in range(32):
            d = c * 32 + n
            rows = gf.at[pl.ds(d * rows_in, rows_in), :]
            for i in range(0, cap, TABLES):
                run = [*zip(tabs, range(i, min(i + TABLES, cap)))]
                at = [pl.ds(idx_s[k][d], 1) for _, k in run]
                new = [t[here, :] + rows[k:k + 1, :] for (t, k), here in zip(run, at)]
                for (t, _), here, value in zip(run, at, new):
                    t[here, :] = value
        return carry
    lax.fori_loop(0, devices // 32, add, 0)
    load_state.wait()

    per = 32

    def measure(c, carry):
        means = []
        for k in range(per):
            rows = pl.ds(pl.multiple_of((c * per + k) * LANES, LANES), LANES)
            total = functools.reduce(jnp.add, [t[rows, :] for t in tabs])
            tabs[0][rows, :] = total
            square = total * total
            high = square.astype(BF16)
            low = (square - high.astype(F32)).astype(BF16)
            both = lax.dot_general(
                jnp.ones((8, 2 * columns), BF16), jnp.concatenate([high, low], axis=1),
                (((1,), (1,)), ((), ())), preferred_element_type=F32,
            )
            means.append(both[0:1, :])
        here = pl.ds(pl.multiple_of(c * per, per), per)
        state = state_ref[here, :] + jnp.concatenate(means, axis=0) * (1.0 / columns)
        nstate[here, :] = state
        scales[here, :] = 0.5 / jnp.sqrt(state)
        return carry
    lax.fori_loop(0, owned // (per * LANES), measure, 0)
    out_state = pltpu.make_async_copy(nstate, nstate_hbm, sems.at[3])
    out_state.start()
    load.wait()

    cols_v[:, 0:owned // LANES] = jnp.transpose(scales[...])
    def update(c, carry):
        for k in range(16):
            rows = pl.ds(pl.multiple_of((c * 16 + k) * LANES, LANES), LANES)
            emb[rows, :] = emb[rows, :] - tabs[0][rows, :] * pick(cols_v[...], c * 16 + k)
        rows = pl.ds(pl.multiple_of(c * 16 * LANES, 16 * LANES), 16 * LANES)
        pltpu.make_async_copy(emb.at[rows, :], nemb_hbm.at[rows, :], sems.at[2]).start()
        return carry
    lax.fori_loop(0, owned // (16 * LANES), update, 0)

    copies[1].wait()

    def fetch(c, carry):
        for n in range(16):
            d = c * 16 + n
            rows = gf.at[pl.ds(pl.multiple_of(d * cap, cap), cap), :]
            for i in range(cap):
                rows[i:i + 1, :] = emb[pl.ds(idx_s[cap + i][d], 1), :]
        return carry
    lax.fori_loop(0, devices // 16, fetch, 0)
    ret_ref[...] = gf[0:devices * cap, :].astype(BF16)
    out_state.wait()
    pltpu.make_async_copy(emb, nemb_hbm, sems.at[2]).wait()


def unpack_kernel(q_any, ret_ref, out_ref, wide, rows, q_ref, sem):
    copy = pltpu.make_async_copy(q_any, q_ref, sem)
    copy.start()
    wide[...] = ret_ref[...].astype(F32)
    copy.wait()

    def take(i, carry):
        for u in range(16):
            for b in range(q_ref.shape[0]):
                rows[pl.ds(b * LANES + i * 16 + u, 1), :] = wide[pl.ds(q_ref.at[b][i * 16 + u], 1), :]
        return carry
    lax.fori_loop(0, LANES // 16, take, 0)
    out_ref[...] = rows[...].astype(BF16)


VM = pl.BlockSpec(memory_space=pltpu.VMEM)
ANY = pl.BlockSpec(memory_space=pl.ANY)


def on_device(owners, offsets, gradients, embedding, adagrad_state, next_owners, next_offsets):
    devices = lax.axis_size(AXES)
    lookups, columns = gradients.shape
    owned = embedding.shape[0]
    cap = max(2, 4 * lookups // devices)
    rows_out = cap + 2
    blocks = lookups // LANES
    shape = jax.ShapeDtypeStruct
    view = lambda x: x.reshape(blocks, LANES)
    in_hbm = lambda x: pltpu.with_memory_space_constraint(x, pltpu.HBM)

    outgoing, q = pl.pallas_call(
        functools.partial(pack_kernel, cap, rows_out),
        out_shape=(shape((devices * rows_out, columns), BF16), shape((blocks, LANES), I32)),
        in_specs=[ANY] * 5,
        out_specs=(VM, VM),
        scratch_shapes=[pltpu.VMEM((blocks, LANES), I32)] * 4
        + [
            pltpu.VMEM((lookups, columns), BF16),
            pltpu.VMEM((lookups, columns), F32),
            pltpu.VMEM((devices * rows_out, columns), F32),
            pltpu.VMEM((blocks, LANES), I32),
            pltpu.SMEM((blocks, LANES), I32),
            pltpu.SemaphoreType.DMA((6,)),
        ],
        compiler_params=pltpu.CompilerParams(vmem_limit_bytes=12 << 20),
        name="pack",
    )(*map(in_hbm, (view(owners), view(offsets), view(next_owners), view(next_offsets), gradients)))

    def exchange(x, pairs):
        x = x.reshape(devices, pairs, 2, columns)
        x = lax.all_to_all(x, AXES, split_axis=0, concat_axis=0, tiled=True)
        return x.reshape(devices * pairs * 2, columns)

    incoming = exchange(outgoing, rows_out // 2)

    new_embedding, new_state, fetched = pl.pallas_call(
        functools.partial(owner_kernel, cap, rows_out),
        out_shape=(
            shape(embedding.shape, F32),
            shape((owned // LANES, LANES), F32),
            shape((devices * cap, columns), BF16),
        ),
        in_specs=[VM, ANY, ANY],
        out_specs=(ANY, ANY, VM),
        scratch_shapes=[
            pltpu.VMEM((devices * rows_out, columns), F32),
            pltpu.VMEM((LANES, devices), I32),
            pltpu.VMEM((LANES, LANES), F32),
            pltpu.VMEM((owned, columns), F32),
            pltpu.VMEM((owned // LANES, LANES), F32),
            pltpu.VMEM((owned // LANES, LANES), F32),
            pltpu.VMEM((owned // LANES, LANES), F32),
            pltpu.SemaphoreType.DMA((6,)),
            pltpu.SMEM((2 * cap, devices), I32),
        ] + [pltpu.VMEM((owned, columns), F32)] * TABLES,
        compiler_params=pltpu.CompilerParams(vmem_limit_bytes=36 << 20),
        name="owner",
    )(incoming, in_hbm(adagrad_state.reshape(owned // LANES, LANES)), in_hbm(embedding))

    returned = lax.all_to_all(
        fetched.reshape(devices, cap, columns), AXES, split_axis=0, concat_axis=0, tiled=True
    ).reshape(devices * cap, columns)

    next_rows = pl.pallas_call(
        unpack_kernel,
        out_shape=shape((lookups, columns), BF16),
        in_specs=[ANY, VM],
        out_specs=VM,
        scratch_shapes=[
            pltpu.VMEM((devices * cap, columns), F32),
            pltpu.VMEM((lookups, columns), F32),
            pltpu.SMEM((blocks, LANES), I32),
            pltpu.SemaphoreType.DMA,
        ],
        compiler_params=pltpu.CompilerParams(vmem_limit_bytes=12 << 20),
        name="unpack",
    )(q, returned)
    return (new_embedding, new_state.reshape(owned), next_rows)


def solution(mesh):
    line, block = P(AXES), P(AXES, None)
    return jax.shard_map(
        on_device,
        mesh=mesh,
        in_specs=(block, line, block, block, line, block, line),
        out_specs=(block, line, block),
        check_vma=False,
    )
```

```python
import functools

import jax
import jax.numpy as jnp
from jax import lax
from jax.experimental import pallas as pl
from jax.experimental.pallas import tpu as pltpu
from jax.sharding import PartitionSpec as P

AXES = ("dp", "rows")
F32, BF16, I32 = jnp.float32, jnp.bfloat16, jnp.int32
LANES = 128
TABLES = 4


def iota(shape, dim):
    return lax.broadcasted_iota(I32, shape, dim)


def pack_kernel(cap, rows_out, own_hbm, off_hbm, nown_hbm, noff_hbm, g_hbm, out_ref, q_ref,
                own_ref, off_ref, nown_ref, noff_ref, g_ref, gf, outf, pos_v, pos_s, sems):
    loads = [
        pltpu.make_async_copy(src, dst, sems.at[k])
        for k, (src, dst) in enumerate((
            (own_hbm, own_ref), (off_hbm, off_ref), (nown_hbm, nown_ref), (noff_hbm, noff_ref), (g_hbm, g_ref)
        ))
    ]
    for load in loads:
        load.start()
    outf[...] = jnp.zeros_like(outf)
    blocks = own_ref.shape[0]
    devices = out_ref.shape[0] // rows_out
    counts = jnp.concatenate(
        [(iota((LANES, LANES), 0) < iota((LANES, LANES), 1)).astype(BF16), jnp.ones((LANES, LANES), BF16)], axis=1
    )
    row = iota((2 * cap, LANES), 0)
    name = iota((devices, LANES), 0).astype(F32).astype(BF16)

    def slots(o_ref, f_ref):
        base = jnp.zeros((devices, LANES), F32)
        out, hots, sels = [], [], []
        for b in range(blocks):
            own = o_ref[b:b + 1, :]
            hot = jnp.where(name == own.astype(F32).astype(BF16), jnp.bfloat16(1), jnp.bfloat16(0))
            count = jnp.dot(hot, counts, preferred_element_type=F32)
            ahead = (count[:, 0:LANES] + base).astype(BF16)
            slot = jnp.sum((hot * ahead).astype(F32), axis=0, keepdims=True).astype(I32)
            base = base + count[:, LANES:]
            off = f_ref[b:b + 1, :]
            value = jnp.where(row < cap, off // LANES + 1, off % LANES)
            sel = jnp.where(row % cap == slot, value, 0).astype(F32).astype(BF16)
            hots.append(hot)
            sels.append(sel)
            out.append((own, slot))
        meta = lax.dot_general(
            jnp.concatenate(hots, axis=1), jnp.concatenate(sels, axis=1), (((1,), (1,)), ((), ())),
            preferred_element_type=F32,
        )
        return out, meta

    loads[0].wait()
    loads[1].wait()
    got, sent = slots(own_ref, off_ref)
    for b, (own, slot) in enumerate(got):
        pos_v[b:b + 1, :] = own * rows_out + slot
    copy = pltpu.make_async_copy(pos_v, pos_s, sems.at[5])
    copy.start()
    for load in loads[2:]:
        load.wait()
    gf[...] = g_ref[...].astype(F32)
    got, asked = slots(nown_ref, noff_ref)
    for b, (own, slot) in enumerate(got):
        q_ref[b:b + 1, :] = own * cap + slot
    outf[pl.ds(cap, devices, stride=rows_out), :] = jnp.concatenate([sent, asked], axis=1)
    copy.wait()

    def place(i, carry):
        for u in range(32):
            for b in range(blocks):
                outf[pl.ds(pos_s.at[b][i * 32 + u], 1), :] = gf[pl.ds(b * LANES + i * 32 + u, 1), :]
        return carry
    lax.fori_loop(0, LANES // 32, place, 0)
    out_ref[...] = outf[...].astype(BF16)


def pick(x, lane):
    return jnp.take_along_axis(x, jnp.full(x.shape, lane, I32), axis=1)


def owner_kernel(cap, rows_in, inc_ref, state_hbm, emb_hbm, nemb_hbm, nstate_hbm, ret_ref,
                 gf, idx_v, cols_v, emb, state_ref, nstate, scales, sems, idx_all, *tabs):
    devices = idx_v.shape[1]
    owned, columns = emb.shape
    gf[...] = inc_ref[...].astype(F32)
    m = gf[pl.ds(cap, devices, stride=rows_in), :]
    index = ((m - 1.0) * LANES + pltpu.roll(m, LANES - cap, 1)).astype(I32)
    apart = iota((devices, LANES), 0) * cap + iota((devices, LANES), 1) % cap
    idx_v[...] = jnp.transpose(jnp.where(index < 0, apart % owned, index))
    copies = [
        pltpu.make_async_copy(idx_v.at[pl.ds(2 * cap * k, cap), :], idx_all.at[pl.ds(cap * k, cap), :], sems.at[k + 4])
        for k in range(2)
    ]
    for copy in copies:
        copy.start()
    idx_s = [idx_all.at[i] for i in range(2 * cap)]
    load = pltpu.make_async_copy(emb_hbm, emb, sems.at[0])
    load.start()
    load_state = pltpu.make_async_copy(state_hbm, state_ref, sems.at[3])
    load_state.start()

    def clear(c, carry):
        for t in tabs:
            t[pl.ds(pl.multiple_of(c * 256, 256), 256), :] = jnp.zeros((256, columns), F32)
        return carry
    lax.fori_loop(0, owned // 256, clear, 0)
    copies[0].wait()

    def add(c, carry):
        for n in range(32):
            d = c * 32 + n
            rows = gf.at[pl.ds(d * rows_in, rows_in), :]
            for i in range(0, cap, TABLES):
                run = [*zip(tabs, range(i, min(i + TABLES, cap)))]
                at = [pl.ds(idx_s[k][d], 1) for _, k in run]
                new = [t[here, :] + rows[k:k + 1, :] for (t, k), here in zip(run, at)]
                for (t, _), here, value in zip(run, at, new):
                    t[here, :] = value
        return carry
    lax.fori_loop(0, devices // 32, add, 0)
    load_state.wait()

    eye = iota((LANES, LANES), 0) == iota((LANES, LANES), 1)
    per = 32

    def measure(c, carry):
        means = []
        for k in range(per):
            rows = pl.ds(pl.multiple_of((c * per + k) * LANES, LANES), LANES)
            total = functools.reduce(jnp.add, [t[rows, :] for t in tabs])
            tabs[0][rows, :] = total
            square = total * total
            if k % 2:
                mean = jnp.sum(square, axis=1, keepdims=True)
                means.append(jnp.sum(jnp.where(eye, mean, 0.0), axis=0, keepdims=True))
            else:
                high = square.astype(BF16)
                low = (square - high.astype(F32)).astype(BF16)
                both = lax.dot_general(
                    jnp.ones((8, 2 * columns), BF16), jnp.concatenate([high, low], axis=1),
                    (((1,), (1,)), ((), ())), preferred_element_type=F32,
                )
                means.append(both[0:1, :])
        here = pl.ds(pl.multiple_of(c * per, per), per)
        state = state_ref[here, :] + jnp.concatenate(means, axis=0) * (1.0 / columns)
        nstate[here, :] = state
        scales[here, :] = 0.5 / jnp.sqrt(state)
        return carry
    lax.fori_loop(0, owned // (per * LANES), measure, 0)
    out_state = pltpu.make_async_copy(nstate, nstate_hbm, sems.at[3])
    out_state.start()
    load.wait()

    cols_v[:, 0:owned // LANES] = jnp.transpose(scales[...])
    def update(c, carry):
        for k in range(32):
            rows = pl.ds(pl.multiple_of((c * 32 + k) * LANES, LANES), LANES)
            emb[rows, :] = emb[rows, :] - tabs[0][rows, :] * pick(cols_v[...], c * 32 + k)
        rows = pl.ds(pl.multiple_of(c * 32 * LANES, 32 * LANES), 32 * LANES)
        pltpu.make_async_copy(emb.at[rows, :], nemb_hbm.at[rows, :], sems.at[2]).start()
        return carry
    lax.fori_loop(0, owned // (32 * LANES), update, 0)

    copies[1].wait()

    def fetch(c, carry):
        for n in range(16):
            d = c * 16 + n
            rows = gf.at[pl.ds(pl.multiple_of(d * cap, cap), cap), :]
            for i in range(cap):
                rows[i:i + 1, :] = emb[pl.ds(idx_s[cap + i][d], 1), :]
        return carry
    lax.fori_loop(0, devices // 16, fetch, 0)
    ret_ref[...] = gf[0:devices * cap, :].astype(BF16)
    out_state.wait()
    pltpu.make_async_copy(emb, nemb_hbm, sems.at[2]).wait()


def unpack_kernel(q_any, ret_ref, out_ref, wide, rows, q_ref, sem):
    copy = pltpu.make_async_copy(q_any, q_ref, sem)
    copy.start()
    wide[...] = ret_ref[...].astype(F32)
    copy.wait()

    def take(i, carry):
        for u in range(32):
            for b in range(q_ref.shape[0]):
                rows[pl.ds(b * LANES + i * 32 + u, 1), :] = wide[pl.ds(q_ref.at[b][i * 32 + u], 1), :]
        return carry
    lax.fori_loop(0, LANES // 32, take, 0)
    out_ref[...] = rows[...].astype(BF16)


VM = pl.BlockSpec(memory_space=pltpu.VMEM)
ANY = pl.BlockSpec(memory_space=pl.ANY)


def on_device(owners, offsets, gradients, embedding, adagrad_state, next_owners, next_offsets):
    devices = lax.axis_size(AXES)
    lookups, columns = gradients.shape
    owned = embedding.shape[0]
    cap = max(2, 4 * lookups // devices)
    rows_out = cap + 2
    blocks = lookups // LANES
    shape = jax.ShapeDtypeStruct
    view = lambda x: x.reshape(blocks, LANES)
    in_hbm = lambda x: pltpu.with_memory_space_constraint(x, pltpu.HBM)

    outgoing, q = pl.pallas_call(
        functools.partial(pack_kernel, cap, rows_out),
        out_shape=(shape((devices * rows_out, columns), BF16), shape((blocks, LANES), I32)),
        in_specs=[ANY] * 5,
        out_specs=(VM, VM),
        scratch_shapes=[pltpu.VMEM((blocks, LANES), I32)] * 4
        + [
            pltpu.VMEM((lookups, columns), BF16),
            pltpu.VMEM((lookups, columns), F32),
            pltpu.VMEM((devices * rows_out, columns), F32),
            pltpu.VMEM((blocks, LANES), I32),
            pltpu.SMEM((blocks, LANES), I32),
            pltpu.SemaphoreType.DMA((6,)),
        ],
        compiler_params=pltpu.CompilerParams(vmem_limit_bytes=12 << 20),
        name="pack",
    )(*map(in_hbm, (view(owners), view(offsets), view(next_owners), view(next_offsets), gradients)))

    def exchange(x, pairs):
        x = x.reshape(devices, pairs, 2, columns)
        x = lax.all_to_all(x, AXES, split_axis=0, concat_axis=0, tiled=True)
        return x.reshape(devices * pairs * 2, columns)

    incoming = exchange(outgoing, rows_out // 2)

    new_embedding, new_state, fetched = pl.pallas_call(
        functools.partial(owner_kernel, cap, rows_out),
        out_shape=(
            shape(embedding.shape, F32),
            shape((owned // LANES, LANES), F32),
            shape((devices * cap, columns), BF16),
        ),
        in_specs=[VM, ANY, ANY],
        out_specs=(ANY, ANY, VM),
        scratch_shapes=[
            pltpu.VMEM((devices * rows_out, columns), F32),
            pltpu.VMEM((LANES, devices), I32),
            pltpu.VMEM((LANES, LANES), F32),
            pltpu.VMEM((owned, columns), F32),
            pltpu.VMEM((owned // LANES, LANES), F32),
            pltpu.VMEM((owned // LANES, LANES), F32),
            pltpu.VMEM((owned // LANES, LANES), F32),
            pltpu.SemaphoreType.DMA((6,)),
            pltpu.SMEM((2 * cap, devices), I32),
        ] + [pltpu.VMEM((owned, columns), F32)] * TABLES,
        compiler_params=pltpu.CompilerParams(vmem_limit_bytes=36 << 20),
        name="owner",
    )(incoming, in_hbm(adagrad_state.reshape(owned // LANES, LANES)), in_hbm(embedding))

    returned = lax.all_to_all(
        fetched.reshape(devices, cap, columns), AXES, split_axis=0, concat_axis=0, tiled=True
    ).reshape(devices * cap, columns)

    next_rows = pl.pallas_call(
        unpack_kernel,
        out_shape=shape((lookups, columns), BF16),
        in_specs=[ANY, VM],
        out_specs=VM,
        scratch_shapes=[
            pltpu.VMEM((devices * cap, columns), F32),
            pltpu.VMEM((lookups, columns), F32),
            pltpu.SMEM((blocks, LANES), I32),
            pltpu.SemaphoreType.DMA,
        ],
        compiler_params=pltpu.CompilerParams(vmem_limit_bytes=12 << 20),
        name="unpack",
    )(q, returned)
    return (new_embedding, new_state.reshape(owned), next_rows)


def solution(mesh):
    line, block = P(AXES), P(AXES, None)
    return jax.shard_map(
        on_device,
        mesh=mesh,
        in_specs=(block, line, block, block, line, block, line),
        out_specs=(block, line, block),
        check_vma=False,
    )
```

```python
import functools

import jax
import jax.numpy as jnp
from jax import lax
from jax.experimental import pallas as pl
from jax.experimental.pallas import tpu as pltpu
from jax.sharding import PartitionSpec as P

AXES = ("dp", "rows")
F32, BF16, I32 = jnp.float32, jnp.bfloat16, jnp.int32
LANES = 128
TABLES = 4


def iota(shape, dim):
    return lax.broadcasted_iota(I32, shape, dim)


def pack_kernel(cap, rows_out, own_hbm, off_hbm, nown_hbm, noff_hbm, g_hbm, out_ref, q_ref,
                t0, t1, own_ref, off_ref, nown_ref, noff_ref, g_ref, gf, outf, pos_v, pos_s, sems):
    loads = [
        pltpu.make_async_copy(src, dst, sems.at[k])
        for k, (src, dst) in enumerate((
            (own_hbm, own_ref), (off_hbm, off_ref), (nown_hbm, nown_ref), (noff_hbm, noff_ref), (g_hbm, g_ref)
        ))
    ]
    for load in loads:
        load.start()
    outf[...] = jnp.zeros_like(outf)

    def clear(c, carry):
        for t in (t0, t1):
            t[pl.ds(pl.multiple_of(c * 256, 256), 256), :] = jnp.zeros((256, t.shape[1]), F32)
        return carry
    lax.fori_loop(0, t0.shape[0] // 256, clear, 0)
    blocks = own_ref.shape[0]
    devices = out_ref.shape[0] // rows_out
    counts = jnp.concatenate(
        [(iota((LANES, LANES), 0) < iota((LANES, LANES), 1)).astype(BF16), jnp.ones((LANES, LANES), BF16)], axis=1
    )
    row = iota((2 * cap, LANES), 0)
    name = iota((devices, LANES), 0).astype(F32).astype(BF16)

    def slots(o_ref, f_ref):
        base = jnp.zeros((devices, LANES), F32)
        out, hots, sels = [], [], []
        for b in range(blocks):
            own = o_ref[b:b + 1, :]
            hot = jnp.where(name == own.astype(F32).astype(BF16), jnp.bfloat16(1), jnp.bfloat16(0))
            count = jnp.dot(hot, counts, preferred_element_type=F32)
            ahead = (count[:, 0:LANES] + base).astype(BF16)
            slot = jnp.sum((hot * ahead).astype(F32), axis=0, keepdims=True).astype(I32)
            base = base + count[:, LANES:]
            off = f_ref[b:b + 1, :]
            value = jnp.where(row < cap, off // LANES + 1, off % LANES)
            sel = jnp.where(row % cap == slot, value, 0).astype(F32).astype(BF16)
            hots.append(hot)
            sels.append(sel)
            out.append((own, slot))
        meta = lax.dot_general(
            jnp.concatenate(hots, axis=1), jnp.concatenate(sels, axis=1), (((1,), (1,)), ((), ())),
            preferred_element_type=F32,
        )
        return out, meta

    loads[0].wait()
    loads[1].wait()
    got, sent = slots(own_ref, off_ref)
    for b, (own, slot) in enumerate(got):
        pos_v[b:b + 1, :] = own * rows_out + slot
    copy = pltpu.make_async_copy(pos_v, pos_s, sems.at[5])
    copy.start()
    for load in loads[2:]:
        load.wait()
    gf[...] = g_ref[...].astype(F32)
    got, asked = slots(nown_ref, noff_ref)
    for b, (own, slot) in enumerate(got):
        q_ref[b:b + 1, :] = own * cap + slot
    outf[pl.ds(cap, devices, stride=rows_out), :] = jnp.concatenate([sent, asked], axis=1)
    copy.wait()

    def place(i, carry):
        for u in range(16):
            for b in range(blocks):
                outf[pl.ds(pos_s.at[b][i * 16 + u], 1), :] = gf[pl.ds(b * LANES + i * 16 + u, 1), :]
        return carry
    lax.fori_loop(0, LANES // 16, place, 0)
    out_ref[...] = outf[...].astype(BF16)


def pick(x, lane):
    return jnp.take_along_axis(x, jnp.full(x.shape, lane, I32), axis=1)


def owner_kernel(cap, rows_in, inc_ref, state_hbm, emb_hbm, _0, _1, nemb_hbm, nstate_hbm, ret_ref,
                 t0, t1, gf, idx_v, cols_v, emb, state_ref, nstate, scales, sems, idx_all, *more):
    devices = idx_v.shape[1]
    owned, columns = emb.shape
    tabs = (t0, t1, *more)
    gf[...] = inc_ref[...].astype(F32)
    m = gf[pl.ds(cap, devices, stride=rows_in), :]
    index = ((m - 1.0) * LANES + pltpu.roll(m, LANES - cap, 1)).astype(I32)
    apart = iota((devices, LANES), 0) * cap + iota((devices, LANES), 1) % cap
    idx_v[...] = jnp.transpose(jnp.where(index < 0, apart % owned, index))
    copies = [
        pltpu.make_async_copy(idx_v.at[pl.ds(2 * cap * k, cap), :], idx_all.at[pl.ds(cap * k, cap), :], sems.at[k + 4])
        for k in range(2)
    ]
    for copy in copies:
        copy.start()
    idx_s = [idx_all.at[i] for i in range(2 * cap)]
    load = pltpu.make_async_copy(emb_hbm, emb, sems.at[0])
    load.start()
    load_state = pltpu.make_async_copy(state_hbm, state_ref, sems.at[3])
    load_state.start()

    def clear(c, carry):
        for t in more:
            t[pl.ds(pl.multiple_of(c * 256, 256), 256), :] = jnp.zeros((256, columns), F32)
        return carry
    lax.fori_loop(0, owned // 256, clear, 0)
    copies[0].wait()

    def add(c, carry):
        for n in range(32):
            d = c * 32 + n
            rows = gf.at[pl.ds(d * rows_in, rows_in), :]
            for i in range(0, cap, TABLES):
                run = [*zip(tabs, range(i, min(i + TABLES, cap)))]
                at = [pl.ds(idx_s[k][d], 1) for _, k in run]
                new = [t[here, :] + rows[k:k + 1, :] for (t, k), here in zip(run, at)]
                for (t, _), here, value in zip(run, at, new):
                    t[here, :] = value
        return carry
    lax.fori_loop(0, devices // 32, add, 0)
    load_state.wait()

    per = 32

    def measure(c, carry):
        means = []
        for k in range(per):
            rows = pl.ds(pl.multiple_of((c * per + k) * LANES, LANES), LANES)
            total = functools.reduce(jnp.add, [t[rows, :] for t in tabs])
            tabs[0][rows, :] = total
            square = total * total
            high = square.astype(BF16)
            low = (square - high.astype(F32)).astype(BF16)
            both = lax.dot_general(
                jnp.ones((8, 2 * columns), BF16), jnp.concatenate([high, low], axis=1),
                (((1,), (1,)), ((), ())), preferred_element_type=F32,
            )
            means.append(both[0:1, :])
        here = pl.ds(pl.multiple_of(c * per, per), per)
        state = state_ref[here, :] + jnp.concatenate(means, axis=0) * (1.0 / columns)
        nstate[here, :] = state
        scales[here, :] = 0.5 / jnp.sqrt(state)
        return carry
    lax.fori_loop(0, owned // (per * LANES), measure, 0)
    out_state = pltpu.make_async_copy(nstate, nstate_hbm, sems.at[3])
    out_state.start()
    load.wait()

    cols_v[:, 0:owned // LANES] = jnp.transpose(scales[...])
    def update(c, carry):
        for k in range(16):
            rows = pl.ds(pl.multiple_of((c * 16 + k) * LANES, LANES), LANES)
            emb[rows, :] = emb[rows, :] - tabs[0][rows, :] * pick(cols_v[...], c * 16 + k)
        rows = pl.ds(pl.multiple_of(c * 16 * LANES, 16 * LANES), 16 * LANES)
        pltpu.make_async_copy(emb.at[rows, :], nemb_hbm.at[rows, :], sems.at[2]).start()
        return carry
    lax.fori_loop(0, owned // (16 * LANES), update, 0)

    copies[1].wait()

    def fetch(c, carry):
        for n in range(16):
            d = c * 16 + n
            rows = gf.at[pl.ds(pl.multiple_of(d * cap, cap), cap), :]
            for i in range(cap):
                rows[i:i + 1, :] = emb[pl.ds(idx_s[cap + i][d], 1), :]
        return carry
    lax.fori_loop(0, devices // 16, fetch, 0)
    ret_ref[...] = gf[0:devices * cap, :].astype(BF16)
    out_state.wait()
    pltpu.make_async_copy(emb, nemb_hbm, sems.at[2]).wait()


def unpack_kernel(q_any, ret_ref, out_ref, wide, rows, q_ref, sem):
    copy = pltpu.make_async_copy(q_any, q_ref, sem)
    copy.start()
    wide[...] = ret_ref[...].astype(F32)
    copy.wait()

    def take(i, carry):
        for u in range(16):
            for b in range(q_ref.shape[0]):
                rows[pl.ds(b * LANES + i * 16 + u, 1), :] = wide[pl.ds(q_ref.at[b][i * 16 + u], 1), :]
        return carry
    lax.fori_loop(0, LANES // 16, take, 0)
    out_ref[...] = rows[...].astype(BF16)


VM = pl.BlockSpec(memory_space=pltpu.VMEM)
ANY = pl.BlockSpec(memory_space=pl.ANY)


def on_device(owners, offsets, gradients, embedding, adagrad_state, next_owners, next_offsets):
    devices = lax.axis_size(AXES)
    lookups, columns = gradients.shape
    owned = embedding.shape[0]
    cap = max(2, 4 * lookups // devices)
    rows_out = cap + 2
    blocks = lookups // LANES
    shape = jax.ShapeDtypeStruct
    view = lambda x: x.reshape(blocks, LANES)
    in_hbm = lambda x: pltpu.with_memory_space_constraint(x, pltpu.HBM)

    table = pltpu.VMEM((owned, columns), F32)
    outgoing, q, *tables = pl.pallas_call(
        functools.partial(pack_kernel, cap, rows_out),
        out_shape=(shape((devices * rows_out, columns), BF16), shape((blocks, LANES), I32), table, table),
        in_specs=[ANY] * 5,
        out_specs=(VM,) * 4,
        scratch_shapes=[pltpu.VMEM((blocks, LANES), I32)] * 4
        + [
            pltpu.VMEM((lookups, columns), BF16),
            pltpu.VMEM((lookups, columns), F32),
            pltpu.VMEM((devices * rows_out, columns), F32),
            pltpu.VMEM((blocks, LANES), I32),
            pltpu.SMEM((blocks, LANES), I32),
            pltpu.SemaphoreType.DMA((6,)),
        ],
        compiler_params=pltpu.CompilerParams(vmem_limit_bytes=12 << 20),
        name="pack",
    )(*map(in_hbm, (view(owners), view(offsets), view(next_owners), view(next_offsets), gradients)))

    def exchange(x, pairs):
        x = x.reshape(devices, pairs, 2, columns)
        x = lax.all_to_all(x, AXES, split_axis=0, concat_axis=0, tiled=True)
        return x.reshape(devices * pairs * 2, columns)

    incoming = exchange(outgoing, rows_out // 2)

    new_embedding, new_state, fetched = pl.pallas_call(
        functools.partial(owner_kernel, cap, rows_out),
        out_shape=(
            shape(embedding.shape, F32),
            shape((owned // LANES, LANES), F32),
            shape((devices * cap, columns), BF16),
            table,
            table,
        ),
        in_specs=[VM, ANY, ANY, VM, VM],
        out_specs=(ANY, ANY, VM, VM, VM),
        scratch_shapes=[
            pltpu.VMEM((devices * rows_out, columns), F32),
            pltpu.VMEM((LANES, devices), I32),
            pltpu.VMEM((LANES, LANES), F32),
            pltpu.VMEM((owned, columns), F32),
            pltpu.VMEM((owned // LANES, LANES), F32),
            pltpu.VMEM((owned // LANES, LANES), F32),
            pltpu.VMEM((owned // LANES, LANES), F32),
            pltpu.SemaphoreType.DMA((6,)),
            pltpu.SMEM((2 * cap, devices), I32),
        ] + [pltpu.VMEM((owned, columns), F32)] * (TABLES - 2),
        input_output_aliases={3: 3, 4: 4},
        compiler_params=pltpu.CompilerParams(vmem_limit_bytes=24 << 20),
        name="owner",
    )(incoming, in_hbm(adagrad_state.reshape(owned // LANES, LANES)), in_hbm(embedding),
      *[pltpu.with_memory_space_constraint(t, pltpu.VMEM) for t in tables])[:3]

    returned = lax.all_to_all(
        fetched.reshape(devices, cap, columns), AXES, split_axis=0, concat_axis=0, tiled=True
    ).reshape(devices * cap, columns)

    next_rows = pl.pallas_call(
        unpack_kernel,
        out_shape=shape((lookups, columns), BF16),
        in_specs=[ANY, VM],
        out_specs=VM,
        scratch_shapes=[
            pltpu.VMEM((devices * cap, columns), F32),
            pltpu.VMEM((lookups, columns), F32),
            pltpu.SMEM((blocks, LANES), I32),
            pltpu.SemaphoreType.DMA,
        ],
        compiler_params=pltpu.CompilerParams(vmem_limit_bytes=12 << 20),
        name="unpack",
    )(q, returned)
    return (new_embedding, new_state.reshape(owned), next_rows)


def solution(mesh):
    line, block = P(AXES), P(AXES, None)
    return jax.shard_map(
        on_device,
        mesh=mesh,
        in_specs=(block, line, block, block, line, block, line),
        out_specs=(block, line, block),
        check_vma=False,
    )
```

```python
import functools

import jax
import jax.numpy as jnp
from jax import lax
from jax.experimental import pallas as pl
from jax.experimental.pallas import tpu as pltpu
from jax.sharding import PartitionSpec as P

AXES = ("dp", "rows")
F32, BF16, I32 = jnp.float32, jnp.bfloat16, jnp.int32
LANES = 128
TABLES = 4


def iota(shape, dim):
    return lax.broadcasted_iota(I32, shape, dim)


def pack_kernel(cap, rows_out, own_hbm, off_hbm, nown_hbm, noff_hbm, g_hbm, out_ref, q_ref,
                own_ref, off_ref, nown_ref, noff_ref, g_ref, gf, outf, pos_v, pos_s, sems):
    loads = [
        pltpu.make_async_copy(src, dst, sems.at[k])
        for k, (src, dst) in enumerate((
            (own_hbm, own_ref), (off_hbm, off_ref), (nown_hbm, nown_ref), (noff_hbm, noff_ref), (g_hbm, g_ref)
        ))
    ]
    for load in loads:
        load.start()
    outf[...] = jnp.zeros_like(outf)
    blocks = own_ref.shape[0]
    devices = out_ref.shape[0] // rows_out
    counts = jnp.concatenate(
        [(iota((LANES, LANES), 0) < iota((LANES, LANES), 1)).astype(BF16), jnp.ones((LANES, LANES), BF16)], axis=1
    )
    row = iota((2 * cap, LANES), 0)
    name = iota((devices, LANES), 0).astype(F32).astype(BF16)

    def slots(o_ref, f_ref):
        base = jnp.zeros((devices, LANES), F32)
        out, hots, sels = [], [], []
        for b in range(blocks):
            own = o_ref[b:b + 1, :]
            hot = jnp.where(name == own.astype(F32).astype(BF16), jnp.bfloat16(1), jnp.bfloat16(0))
            count = jnp.dot(hot, counts, preferred_element_type=F32)
            ahead = (count[:, 0:LANES] + base).astype(BF16)
            slot = jnp.sum((hot * ahead).astype(F32), axis=0, keepdims=True).astype(I32)
            base = base + count[:, LANES:]
            off = f_ref[b:b + 1, :]
            value = jnp.where(row < cap, off // LANES + 1, off % LANES)
            sel = jnp.where(row % cap == slot, value, 0).astype(F32).astype(BF16)
            hots.append(hot)
            sels.append(sel)
            out.append((own, slot))
        meta = lax.dot_general(
            jnp.concatenate(hots, axis=1), jnp.concatenate(sels, axis=1), (((1,), (1,)), ((), ())),
            preferred_element_type=F32,
        )
        return out, meta

    loads[0].wait()
    loads[1].wait()
    got, sent = slots(own_ref, off_ref)
    for b, (own, slot) in enumerate(got):
        pos_v[b:b + 1, :] = own * rows_out + slot
    copy = pltpu.make_async_copy(pos_v, pos_s, sems.at[5])
    copy.start()
    for load in loads[2:]:
        load.wait()
    gf[...] = g_ref[...].astype(F32)
    got, asked = slots(nown_ref, noff_ref)
    for b, (own, slot) in enumerate(got):
        q_ref[b:b + 1, :] = own * cap + slot
    outf[pl.ds(cap, devices, stride=rows_out), :] = jnp.concatenate([sent, asked], axis=1)
    copy.wait()

    def place(i, carry):
        for u in range(16):
            for b in range(blocks):
                outf[pl.ds(pos_s.at[b][i * 16 + u], 1), :] = gf[pl.ds(b * LANES + i * 16 + u, 1), :]
        return carry
    lax.fori_loop(0, LANES // 16, place, 0)
    out_ref[...] = outf[...].astype(BF16)


def pick(x, lane):
    return jnp.take_along_axis(x, jnp.full(x.shape, lane, I32), axis=1)


def owner_kernel(cap, rows_in, inc_ref, state_hbm, emb_hbm, nemb_hbm, nstate_hbm, ret_ref,
                 gf, idx_v, cols_v, emb, state_ref, nstate, scales, sems, idx_all, *tabs):
    devices = idx_v.shape[1]
    owned, columns = emb.shape
    gf[...] = inc_ref[...].astype(F32)
    m = gf[pl.ds(cap, devices, stride=rows_in), :]
    index = ((m - 1.0) * LANES + pltpu.roll(m, LANES - cap, 1)).astype(I32)
    apart = iota((devices, LANES), 0) * cap + iota((devices, LANES), 1) % cap
    idx_v[...] = jnp.transpose(jnp.where(index < 0, apart % owned, index))
    copies = [
        pltpu.make_async_copy(idx_v.at[pl.ds(2 * cap * k, cap), :], idx_all.at[pl.ds(cap * k, cap), :], sems.at[k + 4])
        for k in range(2)
    ]
    for copy in copies:
        copy.start()
    idx_s = [idx_all.at[i] for i in range(2 * cap)]
    load = pltpu.make_async_copy(emb_hbm, emb, sems.at[0])
    load.start()
    load_state = pltpu.make_async_copy(state_hbm, state_ref, sems.at[3])
    load_state.start()

    def clear(c, carry):
        for t in tabs:
            t[pl.ds(pl.multiple_of(c * 256, 256), 256), :] = jnp.zeros((256, columns), F32)
        return carry
    lax.fori_loop(0, owned // 256, clear, 0)
    copies[0].wait()

    def add(c, carry):
        for n in range(32):
            d = c * 32 + n
            rows = gf.at[pl.ds(d * rows_in, rows_in), :]
            for i in range(0, cap, TABLES):
                run = [*zip(tabs, range(i, min(i + TABLES, cap)))]
                at = [pl.ds(idx_s[k][d], 1) for _, k in run]
                new = [t[here, :] + rows[k:k + 1, :] for (t, k), here in zip(run, at)]
                for (t, _), here, value in zip(run, at, new):
                    t[here, :] = value
        return carry
    lax.fori_loop(0, devices // 32, add, 0)
    load_state.wait()

    per = 32

    def measure(c, carry):
        means = []
        for k in range(per):
            rows = pl.ds(pl.multiple_of((c * per + k) * LANES, LANES), LANES)
            total = functools.reduce(jnp.add, [t[rows, :] for t in tabs])
            tabs[0][rows, :] = total
            square = total * total
            high = square.astype(BF16)
            low = (square - high.astype(F32)).astype(BF16)
            both = lax.dot_general(
                jnp.ones((8, 2 * columns), BF16), jnp.concatenate([high, low], axis=1),
                (((1,), (1,)), ((), ())), preferred_element_type=F32,
            )
            means.append(both[0:1, :])
        here = pl.ds(pl.multiple_of(c * per, per), per)
        state = state_ref[here, :] + jnp.concatenate(means, axis=0) * (1.0 / columns)
        nstate[here, :] = state
        scales[here, :] = 0.5 / jnp.sqrt(state)
        return carry
    lax.fori_loop(0, owned // (per * LANES), measure, 0)
    out_state = pltpu.make_async_copy(nstate, nstate_hbm, sems.at[3])
    out_state.start()
    load.wait()

    cols_v[:, 0:owned // LANES] = jnp.transpose(scales[...])
    def update(c, carry):
        for k in range(32):
            rows = pl.ds(pl.multiple_of((c * 32 + k) * LANES, LANES), LANES)
            emb[rows, :] = emb[rows, :] - tabs[0][rows, :] * pick(cols_v[...], c * 32 + k)
        rows = pl.ds(pl.multiple_of(c * 32 * LANES, 32 * LANES), 32 * LANES)
        pltpu.make_async_copy(emb.at[rows, :], nemb_hbm.at[rows, :], sems.at[2]).start()
        return carry
    lax.fori_loop(0, owned // (32 * LANES), update, 0)

    copies[1].wait()

    def fetch(c, carry):
        for n in range(16):
            d = c * 16 + n
            rows = gf.at[pl.ds(pl.multiple_of(d * cap, cap), cap), :]
            for i in range(cap):
                rows[i:i + 1, :] = emb[pl.ds(idx_s[cap + i][d], 1), :]
        return carry
    lax.fori_loop(0, devices // 16, fetch, 0)
    ret_ref[...] = gf[0:devices * cap, :].astype(BF16)
    out_state.wait()
    pltpu.make_async_copy(emb, nemb_hbm, sems.at[2]).wait()


def unpack_kernel(q_any, ret_ref, out_ref, wide, rows, q_ref, sem):
    copy = pltpu.make_async_copy(q_any, q_ref, sem)
    copy.start()
    wide[...] = ret_ref[...].astype(F32)
    copy.wait()

    def take(i, carry):
        for u in range(16):
            for b in range(q_ref.shape[0]):
                rows[pl.ds(b * LANES + i * 16 + u, 1), :] = wide[pl.ds(q_ref.at[b][i * 16 + u], 1), :]
        return carry
    lax.fori_loop(0, LANES // 16, take, 0)
    out_ref[...] = rows[...].astype(BF16)


VM = pl.BlockSpec(memory_space=pltpu.VMEM)
ANY = pl.BlockSpec(memory_space=pl.ANY)


def on_device(owners, offsets, gradients, embedding, adagrad_state, next_owners, next_offsets):
    devices = lax.axis_size(AXES)
    lookups, columns = gradients.shape
    owned = embedding.shape[0]
    cap = max(2, 4 * lookups // devices)
    rows_out = cap + 2
    blocks = lookups // LANES
    shape = jax.ShapeDtypeStruct
    view = lambda x: x.reshape(blocks, LANES)
    in_hbm = lambda x: pltpu.with_memory_space_constraint(x, pltpu.HBM)

    outgoing, q = pl.pallas_call(
        functools.partial(pack_kernel, cap, rows_out),
        out_shape=(shape((devices * rows_out, columns), BF16), shape((blocks, LANES), I32)),
        in_specs=[ANY] * 5,
        out_specs=(VM, VM),
        scratch_shapes=[pltpu.VMEM((blocks, LANES), I32)] * 4
        + [
            pltpu.VMEM((lookups, columns), BF16),
            pltpu.VMEM((lookups, columns), F32),
            pltpu.VMEM((devices * rows_out, columns), F32),
            pltpu.VMEM((blocks, LANES), I32),
            pltpu.SMEM((blocks, LANES), I32),
            pltpu.SemaphoreType.DMA((6,)),
        ],
        compiler_params=pltpu.CompilerParams(vmem_limit_bytes=12 << 20),
        name="pack",
    )(*map(in_hbm, (view(owners), view(offsets), view(next_owners), view(next_offsets), gradients)))

    def exchange(x, pairs):
        x = x.reshape(devices, pairs, 2, columns)
        x = lax.all_to_all(x, AXES, split_axis=0, concat_axis=0, tiled=True)
        return x.reshape(devices * pairs * 2, columns)

    incoming = exchange(outgoing, rows_out // 2)

    new_embedding, new_state, fetched = pl.pallas_call(
        functools.partial(owner_kernel, cap, rows_out),
        out_shape=(
            shape(embedding.shape, F32),
            shape((owned // LANES, LANES), F32),
            shape((devices * cap, columns), BF16),
        ),
        in_specs=[VM, ANY, ANY],
        out_specs=(ANY, ANY, VM),
        scratch_shapes=[
            pltpu.VMEM((devices * rows_out, columns), F32),
            pltpu.VMEM((LANES, devices), I32),
            pltpu.VMEM((LANES, LANES), F32),
            pltpu.VMEM((owned, columns), F32),
            pltpu.VMEM((owned // LANES, LANES), F32),
            pltpu.VMEM((owned // LANES, LANES), F32),
            pltpu.VMEM((owned // LANES, LANES), F32),
            pltpu.SemaphoreType.DMA((6,)),
            pltpu.SMEM((2 * cap, devices), I32),
        ] + [pltpu.VMEM((owned, columns), F32)] * TABLES,
        compiler_params=pltpu.CompilerParams(vmem_limit_bytes=36 << 20),
        name="owner",
    )(incoming, in_hbm(adagrad_state.reshape(owned // LANES, LANES)), in_hbm(embedding))

    returned = lax.all_to_all(
        fetched.reshape(devices, cap, columns), AXES, split_axis=0, concat_axis=0, tiled=True
    ).reshape(devices * cap, columns)

    next_rows = pl.pallas_call(
        unpack_kernel,
        out_shape=shape((lookups, columns), BF16),
        in_specs=[ANY, VM],
        out_specs=VM,
        scratch_shapes=[
            pltpu.VMEM((devices * cap, columns), F32),
            pltpu.VMEM((lookups, columns), F32),
            pltpu.SMEM((blocks, LANES), I32),
            pltpu.SemaphoreType.DMA,
        ],
        compiler_params=pltpu.CompilerParams(vmem_limit_bytes=12 << 20),
        name="unpack",
    )(q, returned)
    return (new_embedding, new_state.reshape(owned), next_rows)


def solution(mesh):
    line, block = P(AXES), P(AXES, None)
    return jax.shard_map(
        on_device,
        mesh=mesh,
        in_specs=(block, line, block, block, line, block, line),
        out_specs=(block, line, block),
        check_vma=False,
    )
```
